256 devices in a mesh: shell: 4 (over z_hi, core), blk: 64 (over z_lo, y, x).
Axes of the slice: x: 4, y: 4, z: 8 (z_hi: 2, z_lo: 4; z = z_hi * 4 + z_lo), core: 2. Of those that a mesh axis runs over, the one named last changes fastest.
Arguments:
- strain_spec: bfloat16 [6, 4, 1024, 2, 1024], P(None, 'shell', 'blk'), may hold values from -6 to 6
- order_map: int32 [1024], replicated, may hold values from 0 to 1023, as said below
- viscosity: float32 [4, 1024, 2048], P('shell', 'blk'), may hold values from 0.2 to 5
- radial_weight: float32 [4], P('shell'), may hold values from 0.3 to 3
Outputs:
- stress_spec: bfloat16 [6, 4, 1024, 2, 1024], P(None, 'shell', 'blk')
- integrated: float32 [6, 1024, 2, 1024], P(None, 'blk', None, 'shell')
The draws below stay inside these ranges and needn't reach their ends.
Inputs may be any that keep to these rules, and one draw needn't show every extreme that they name: order_map is a permutation of the orders 0 to 1023; the entries 2i and 2i + 1 hold two orders m and 1023 - m, in either order, so each device's 16 slots hold 8 such pairs.
All inputs are finite; a program needn't handle non-finite values.
Results may differ from the reference program's by a relative error of at most 0.014.
Values may be sent and summed in bfloat16 or wider, within the bound.
A program may use at most 128 MiB of HBM per device.

```python
import math
import jax
import jax.numpy as jnp
from jax import lax

DEGREES = 1024
CYCLES = 1024
POINTS = 2048
COMPS = 6
SHELLS = 4


def draw_order_map(key, part):
    pair_key = jax.random.fold_in(key, 11)
    flip_key = jax.random.fold_in(key, 23)
    lower_order = jax.random.permutation(pair_key, DEGREES // 2).astype(jnp.int32)
    upper_order = DEGREES - 1 - lower_order
    flipped = jax.random.randint(flip_key, (DEGREES // 2,), 0, 2).astype(jnp.int32)
    first_slot = jnp.where(flipped == 1, upper_order, lower_order)
    second_slot = jnp.where(flipped == 1, lower_order, upper_order)
    return jnp.stack([first_slot, second_slot], axis=1).reshape(DEGREES).astype(jnp.int32)


def levels(rng, extent, shards, smallest, largest):
    factor_of = 1.0
    for dim, blocks in shards:
        draws = jax.random.uniform(jax.random.fold_in(jax.random.fold_in(rng, 6), dim), (blocks,), jnp.float32, smallest / len(shards), largest / len(shards))
        factor_of = factor_of * jnp.repeat(jnp.exp(draws), extent[dim] // blocks).reshape((-1,) + (1,) * (len(extent) - 1 - dim))
    return factor_of


def centred(own_key, dims, deviation, limit, split=(), held_as=jnp.bfloat16):
    values = deviation * jax.random.normal(own_key, dims, jnp.float32)
    if split:
        values = values * levels(own_key, dims, split, -0.22, 0.18)
    return jnp.clip(values, -limit, limit).astype(held_as)


def setup_inputs(seed: int = 0) -> dict:
    arg_keys = jax.random.split(jax.random.key(seed), 5)
    return {
        "strain_spec": centred(arg_keys[0], (COMPS, SHELLS, DEGREES, 2, DEGREES), 1.0, 6.0, ((1, 4), (2, 64))),
        "order_map": draw_order_map(jax.random.fold_in(arg_keys[4], 71), 0),
        "viscosity": jnp.clip(jnp.exp(math.log(5.0) - 3.218876 * jax.random.uniform(arg_keys[2], (SHELLS, CYCLES, POINTS), jnp.float32) ** levels(arg_keys[2], (SHELLS, CYCLES, POINTS), ((0, 4), (1, 64)), -0.2, 0.2)), 0.2, 5.0),
        "radial_weight": jnp.clip(jnp.exp(math.log(3.0) - 2.3025851 * jax.random.uniform(arg_keys[3], (SHELLS,), jnp.float32) ** levels(arg_keys[3], (SHELLS,), ((0, 4),), -0.2, 0.2)), 0.3, 3.0),
    }


two_power = 1099511627776.0
inverse_power = 1.0 / 1099511627776.0
log_jump = 40.0 * math.log(2.0)

def cycle_geometry(cycle_count):
    cycle_index = jnp.arange(cycle_count // 2, dtype=jnp.float32)
    colatitude = math.pi * (2.0 * cycle_index + 1.0) / (2.0 * cycle_count)
    return (jnp.cos(colatitude), jnp.log(jnp.sin(colatitude)))

def fejer_weights(cycle_count):
    half_count = cycle_count // 2
    cycle_index = jnp.arange(half_count, dtype=jnp.int32)
    wave_number = jnp.arange(1, half_count + 1, dtype=jnp.int32)
    phase_index = wave_number[:, None] * (2 * cycle_index[None, :] + 1) % (2 * cycle_count)
    angles = phase_index.astype(jnp.float32) * (math.pi / cycle_count)
    wave_float = wave_number.astype(jnp.float32)
    divisor = 4.0 * wave_float * wave_float - 1.0
    series = lax.optimization_barrier(jnp.sum(jnp.cos(angles) / divisor[:, None], axis=0))
    return 2.0 / cycle_count * (1.0 - 2.0 * series)

def legendre_tables(orders, cycle_count, degree_count):
    cosine, log_sine = cycle_geometry(cycle_count)
    order_int = orders.astype(jnp.int32)[:, None]
    order_float = orders.astype(jnp.float32)[:, None]
    counter = jnp.arange(1, degree_count, dtype=jnp.int32)
    counter_float = counter.astype(jnp.float32)
    factors = jnp.where(counter[None, :] <= order_int, jnp.log(1.0 - 0.5 / counter_float)[None, :], 0.0)
    log_start = 0.5 * jnp.log((2.0 * order_float + 1.0) / (4.0 * math.pi)) + 0.5 * lax.optimization_barrier(jnp.sum(factors, axis=1, keepdims=True)) + order_float * log_sine[None, :]
    even_first = order_int % 2 == 0

    def advance(carry_state, degree):
        previous, latest, log_scale = carry_state
        degree_float = degree.astype(jnp.float32)
        below_float = degree_float - 1.0
        coef_first = jnp.sqrt(jnp.maximum(4.0 * degree_float * degree_float - 1.0, 0.0) / jnp.maximum(degree_float * degree_float - order_float * order_float, 1.0))
        coef_second = jnp.sqrt(jnp.maximum(below_float * below_float - order_float * order_float, 0.0) / jnp.maximum(4.0 * below_float * below_float - 1.0, 1.0))
        current = coef_first * (cosine[None, :] * latest - coef_second * previous)
        current = jnp.where(degree == order_int + 1, jnp.sqrt(2.0 * order_float + 3.0) * cosine[None, :] * latest, current)
        current = jnp.where(degree == order_int, 1.0, current)
        current = jnp.where(degree < order_int, 0.0, current)
        result = current * jnp.exp(log_scale)
        too_large = jnp.abs(current) > two_power
        factor = jnp.where(too_large, inverse_power, 1.0)
        next_state = (latest * factor, current * factor, log_scale + jnp.where(too_large, log_jump, 0.0))
        return (next_state, result)

    def pair_step(carry_state, half_degree):
        carry_state, lower_row = advance(carry_state, 2 * half_degree)
        carry_state, upper_row = advance(carry_state, 2 * half_degree + 1)
        even_row = jnp.where(even_first, lower_row, upper_row).astype(jnp.bfloat16)
        odd_row = jnp.where(even_first, upper_row, lower_row).astype(jnp.bfloat16)
        return (carry_state, (even_row, odd_row))
    zero_rows = jnp.zeros((orders.shape[0], cycle_count // 2), jnp.float32)
    initial = (zero_rows, zero_rows, log_start + zero_rows)
    final_state, tables = lax.scan(pair_step, initial, jnp.arange(degree_count // 2, dtype=jnp.int32), unroll=32)
    return tables

def fourier_table(orders_all, point_count):
    longitudes = jnp.arange(point_count, dtype=jnp.int32)
    phase_index = orders_all.astype(jnp.int32)[:, None] * longitudes[None, :] % point_count
    angles = phase_index.astype(jnp.float32) * (2.0 * math.pi / point_count)
    return jnp.stack([jnp.cos(angles), -jnp.sin(angles)], axis=1).astype(jnp.bfloat16)

def synthesize(spectra, tables, orders):
    even_first = (orders % 2 == 0)[None, None, :, None, None]
    paired = spectra.reshape(spectra.shape[:-1] + (spectra.shape[-1] // 2, 2))
    even_part = jnp.where(even_first, paired[..., 0], paired[..., 1]).astype(jnp.float32)
    odd_part = jnp.where(even_first, paired[..., 1], paired[..., 0]).astype(jnp.float32)
    symmetric = jnp.einsum('csmri,imj->csmrj', even_part, tables[0].astype(jnp.float32))
    antisymmetric = jnp.einsum('csmri,imj->csmrj', odd_part, tables[1].astype(jnp.float32))
    north_side = symmetric + antisymmetric
    south_side = symmetric - antisymmetric
    return jnp.concatenate([north_side, jnp.flip(south_side, axis=-1)], axis=-1).astype(jnp.bfloat16)

def analyze(gridded, tables, orders, weights):
    half_count = gridded.shape[-1] // 2
    north_side = gridded[..., :half_count].astype(jnp.float32)
    south_side = jnp.flip(gridded[..., half_count:], axis=-1).astype(jnp.float32)
    even_side = (weights * (north_side + south_side)).astype(jnp.bfloat16).astype(jnp.float32)
    odd_side = (weights * (north_side - south_side)).astype(jnp.bfloat16).astype(jnp.float32)
    even_part = jnp.einsum('csmrj,imj->csmri', even_side, tables[0].astype(jnp.float32))
    odd_part = jnp.einsum('csmrj,imj->csmri', odd_side, tables[1].astype(jnp.float32))
    even_first = (orders % 2 == 0)[None, None, :, None, None]
    low_side = jnp.where(even_first, even_part, odd_part)
    high_side = jnp.where(even_first, odd_part, even_part)
    stacked = jnp.stack([low_side, high_side], axis=-1)
    return stacked.reshape(stacked.shape[:-2] + (2 * stacked.shape[-2],))

def reference(strain_spec, order_map, viscosity, radial_weight):
    component_count, shell_count, slot_count, complex_parts, degree_count = strain_spec.shape
    block_size = math.gcd(DEGREES, 64)
    block_count = slot_count // block_size
    orders_blocked = order_map.reshape(block_count, block_size)
    weights = fejer_weights(CYCLES)
    wave_table = fourier_table(order_map, POINTS).astype(jnp.float32)
    doubling = jnp.where(order_map == 0, 1.0, 2.0).astype(jnp.bfloat16)
    norm_factor = 2.0 * math.pi / POINTS
    blocked = strain_spec.reshape(component_count, shell_count, block_count, block_size, 2, degree_count)
    blocked = blocked.transpose(2, 0, 1, 3, 4, 5)

    def synth_block(packed):
        slot_piece, orders = packed
        return synthesize(slot_piece, legendre_tables(orders, CYCLES, DEGREES), orders)
    fourier = lax.map(synth_block, (blocked, orders_blocked))
    fourier = fourier.transpose(2, 1, 0, 3, 4, 5).reshape(shell_count, component_count, slot_count, 2, CYCLES)

    def cycle_shell(packed):
        gridded, shell_viscosity = packed
        scaled = (gridded * doubling[None, :, None, None]).astype(jnp.float32)
        grid_field = jnp.einsum('cmrj,mrk->cjk', scaled, wave_table)
        stress = (shell_viscosity[None] * grid_field).astype(jnp.bfloat16).astype(jnp.float32)
        spectra = jnp.einsum('cjk,mrk->cmrj', stress, wave_table)
        return (spectra * norm_factor).astype(jnp.bfloat16)
    spectrum = lax.map(cycle_shell, (fourier, viscosity))
    spectrum = spectrum.reshape(shell_count, component_count, block_count, block_size, 2, CYCLES)
    spectrum = spectrum.transpose(2, 1, 0, 3, 4, 5)

    def analysis_block(packed):
        slot_piece, orders = packed
        return analyze(slot_piece, legendre_tables(orders, CYCLES, DEGREES), orders, weights)
    coefficient = lax.map(analysis_block, (spectrum, orders_blocked))
    coefficient = coefficient.transpose(1, 2, 0, 3, 4, 5).reshape(component_count, shell_count, slot_count, 2, degree_count)
    stress_spec = coefficient.astype(jnp.bfloat16)
    integrated = lax.optimization_barrier(jnp.sum(coefficient * radial_weight[None, :, None, None, None], axis=1))
    return (stress_spec, integrated)
```

```python
import functools
import math

import jax
import jax.numpy as jnp
import numpy as np
from jax import lax
from jax.experimental import pallas as pl
from jax.experimental.pallas import tpu as pltpu
from jax.sharding import PartitionSpec as P

F32 = jnp.float32
BF16 = jnp.bfloat16
COMPS = 6
PARTS = 2
ORDERS = 16
DEG = 1024
HALF = 512
BLK = 64
CYC = 16
POINTS = 2048
KH = POINTS // 2
LB = 256
LSTRIDE = LB + 1
TILES = HALF // 128
BIG = 2.0**40
SMALL = 2.0**-40
NT = (((1,), (1,)), ((), ()))


def latitude_constants():
    j = np.arange(HALF, dtype=np.float64)
    theta = np.pi * (2.0 * j + 1.0) / (4.0 * HALF)
    x = np.cos(theta)
    logsin = np.log2(np.sin(theta))
    hi = np.round(logsin * 512.0) / 512.0
    lo = logsin - hi
    k = np.arange(1, HALF + 1, dtype=np.float64)
    phase = np.outer(k, 2.0 * j + 1.0) % (4.0 * HALF)
    series = np.sum(np.cos(phase * np.pi / (2.0 * HALF)) / (4.0 * k * k - 1.0)[:, None], axis=0)
    weight = (2.0 / (2.0 * HALF)) * (1.0 - 2.0 * series)
    m = np.arange(DEG, dtype=np.float64)
    fac = np.concatenate([[0.0], np.cumsum(np.log2(1.0 - 0.5 / np.arange(1, DEG)))])
    g = 0.5 * np.log2((2.0 * m + 1.0) / (4.0 * np.pi)) + 0.5 * fac
    lat = np.stack([x, hi, lo, weight]).astype(np.float32)
    return np.concatenate([lat, np.zeros((4, HALF), np.float32)]), g.astype(np.float32)[None]


def legendre_kernel(ord_ref, mb_ref, lat_ref, g_ref, spec_ref, tab_ref, msg_ref, ca, cab, prev, cur, ini, expo, ft, acc, lhs, ns):
    step = pl.program_id(0)

    @pl.when(step == 0)
    def _():
        lane = lax.broadcasted_iota(jnp.int32, (8, 128), 1).astype(F32)
        glane = lax.broadcasted_iota(jnp.int32, (8, DEG), 1).astype(F32)
        for par in range(2):
            m = mb_ref[par]
            for b in range(DEG // 128):
                l = lane + float(128 * b)
                up = l > m
                den = jnp.where(up, (l - m) * (l + m), 1.0)
                a2 = (4.0 * l * l - 1.0) / den
                a = jnp.where(up, jnp.sqrt(jnp.where(up, a2, 1.0)), 0.0)
                below = l - 1.0
                top = jnp.where(below > m, (below - m) * (below + m), 0.0)
                b2 = top / jnp.maximum(4.0 * below * below - 1.0, 1.0)
                ca[b, par] = a
                cab[b, par] = a * jnp.sqrt(b2)
            gm = jnp.sum(jnp.where(glane == m[:, :1], g_ref[...], 0.0), axis=1, keepdims=True)
            for t in range(TILES):
                cols = pl.ds(128 * t, 128)
                mh = m * lat_ref[1:2, cols]
                whole = jnp.floor(mh)
                frac = (mh - whole) + m * lat_ref[2:3, cols] + gm
                ini[par, t] = jnp.exp(frac * math.log(2.0))
                expo[par, t] = whole
                prev[par, t] = jnp.zeros((8, 128), F32)
                cur[par, t] = jnp.zeros((8, 128), F32)

        deg = lax.broadcasted_iota(jnp.int32, (16, DEG), 1)

        def place(q, _):
            par, p = q // 8, q % 8
            slot = 2 * p + ((ord_ref[2 * p] + par) & 1)
            order = ord_ref[slot]
            rows = [spec_ref[c, slot].astype(F32) for c in range(COMPS)]
            rows.append(jnp.zeros((4, DEG), F32))
            data = jnp.concatenate(rows, axis=0) * jnp.where(order == 0, 1.0, 2.0)
            even = ((deg + order) & 1) == 0
            lhs[q, 0:16] = jnp.where(even, data, 0.0).astype(BF16)
            lhs[q, 16:32] = jnp.where(even, 0.0, data).astype(BF16)
            acc[q] = jnp.zeros((32, HALF), F32)
            return 0

        lax.fori_loop(0, ORDERS, place, 0)

    def eight(sub, _):
        block = step * (LB // 128) + sub // 16
        shift = (128 - 8 * (sub % 16)) % 128
        base = step * LB + sub * 8
        av = [pltpu.roll(ca[block, par], shift, 1) for par in range(2)]
        abv = [pltpu.roll(cab[block, par], shift, 1) for par in range(2)]
        xs = [jnp.broadcast_to(lat_ref[0:1, pl.ds(128 * t, 128)], (8, 128)) for t in range(TILES)]
        for par in range(2):
            m = mb_ref[par]
            state = []
            for t in range(TILES):
                e = expo[par, t]
                c, p = cur[par, t], prev[par, t]
                big = jnp.abs(c) > BIG
                f = jnp.where(big, SMALL, 1.0)
                e = jnp.where(big, e + 40.0, e)
                expo[par, t] = e
                scale = jnp.where(e < -126.0, 0.0, jnp.exp(jnp.maximum(e, -126.0) * math.log(2.0)))
                state.append((p * f, c * f, scale, ini[par, t]))
            for r in range(8):
                a = jnp.broadcast_to(av[par][:, r : r + 1], (8, 128))
                ab = jnp.broadcast_to(abv[par][:, r : r + 1], (8, 128))
                hit = m == (base + r).astype(F32)
                for t in range(TILES):
                    p, c, scale, start = state[t]
                    new = (a * xs[t]) * c - ab * p
                    new = jnp.where(hit, start, new)
                    state[t] = (c, new, scale, start)
                    ft[t, pl.ds(par * 8 * LSTRIDE + sub * 8 + r, 8, stride=LSTRIDE), :] = new * scale
            for t in range(TILES):
                prev[par, t] = state[t][0]
                cur[par, t] = state[t][1]
        return 0

    lax.fori_loop(0, LB // 8, eight, 0)

    for q in range(ORDERS):
        table = jnp.concatenate([ft[t, q * LSTRIDE : q * LSTRIDE + LB, :] for t in range(TILES)], axis=1).astype(BF16)
        tab_ref[q] = table
        left = lhs[q, :, pl.ds(pl.multiple_of(step * LB, LB), LB)]
        acc[q] += jnp.dot(left, table, preferred_element_type=F32)

    @pl.when(step == pl.num_programs(0) - 1)
    def _():
        def spread(q, _):
            sym, anti = acc[q, 0:16], acc[q, 16:32]
            for t in range(TILES):
                cols = slice(128 * t, 128 * t + 128)
                ns[t, pl.ds(q, 16, stride=16), :] = sym[:, cols] + anti[:, cols]
                ns[TILES + t, pl.ds(q, 16, stride=16), :] = sym[:, cols] - anti[:, cols]
            return 0

        lax.fori_loop(0, ORDERS, spread, 0)
        for t in range(2 * TILES):
            flipped = jnp.concatenate([ns[t, 0:128].T, ns[t, 128:256].T], axis=1).astype(BF16)
            for b in range(8):
                d = (t % TILES) * 8 + b
                dest = d if t < TILES else BLK - 1 - d
                msg_ref[dest] = flipped[16 * b : 16 * b + 16]


def run_legendre(my_orders, mb, lat, g, spec):
    full = lambda shape: pl.BlockSpec(shape, lambda i: (0,) * len(shape))
    return pl.pallas_call(
        legendre_kernel,
        grid=(DEG // LB,),
        in_specs=[
            pl.BlockSpec(memory_space=pltpu.SMEM),
            full((2, 8, 128)),
            full((8, HALF)),
            full((1, DEG)),
            full((COMPS, ORDERS, PARTS, DEG)),
        ],
        out_specs=[
            pl.BlockSpec((ORDERS, LB, HALF), lambda i: (0, i, 0)),
            full((BLK, CYC, 256)),
        ],
        out_shape=[
            jax.ShapeDtypeStruct((ORDERS, DEG, HALF), BF16),
            jax.ShapeDtypeStruct((BLK, CYC, 256), BF16),
        ],
        scratch_shapes=[
            pltpu.VMEM((DEG // 128, 2, 8, 128), F32),
            pltpu.VMEM((DEG // 128, 2, 8, 128), F32),
            pltpu.VMEM((2, TILES, 8, 128), F32),
            pltpu.VMEM((2, TILES, 8, 128), F32),
            pltpu.VMEM((2, TILES, 8, 128), F32),
            pltpu.VMEM((2, TILES, 8, 128), F32),
            pltpu.VMEM((TILES, ORDERS * LSTRIDE + 8, 128), F32),
            pltpu.VMEM((ORDERS, 32, HALF), F32),
            pltpu.VMEM((ORDERS, 32, DEG), BF16),
            pltpu.VMEM((2 * TILES, 256, 128), F32),
        ],
        name="legendre",
    )(my_orders, mb, lat, g, spec)


def turn(phase):
    t = phase * (1.0 / KH) - 1.0
    z = t * t
    c = jnp.full_like(z, 0.0)
    s = jnp.full_like(z, 0.0)
    for i in range(8, -1, -1):
        c = c * z + float((-1) ** (i + 1) * math.pi ** (2 * i) / math.factorial(2 * i))
        s = s * z + float((-1) ** (i + 1) * math.pi ** (2 * i + 1) / math.factorial(2 * i + 1))
    return c, s * t


def wrap(value):
    return value - POINTS * jnp.floor(value * (1.0 / POINTS))


def longitude_kernel(flip_ref, me_ref, shift_ref, vis_ref, msg_ref, out_ref, wave, left, pm, spect, vis):
    lane = lax.broadcasted_iota(jnp.int32, (8, 128), 1).astype(F32)
    sc, ss = [], []
    for u in range(KH // 128):
        sc.append(jnp.broadcast_to(shift_ref[0:1, pl.ds(128 * u, 128)], (8, 128)))
        ss.append(jnp.broadcast_to(shift_ref[1:2, pl.ds(128 * u, 128)], (8, 128)))

    def make(src, _):
        m = me_ref[src]
        c, s = turn(wrap(m * lane))
        gc, gs = turn(wrap(m * 128.0))
        for u in range(KH // 128):
            oc = sc[u] * c - ss[u] * s
            os = -(ss[u] * c + sc[u] * s)
            rows = pl.ds(pl.multiple_of(src * 32, 32), 32)
            wave[rows, pl.ds(128 * u, 128)] = jnp.concatenate([c, oc, -s, -os], axis=0).astype(BF16)
            c, s = c * gc - s * gs, s * gc + c * gs
        return 0

    lax.fori_loop(0, BLK, make, 0)

    flip = flip_ref[0]
    for j in range(CYC):
        row = jnp.where(flip == 1, CYC - 1 - j, j)
        vis[j : j + 1, :] = vis_ref[pl.ds(row, 1), :]

    wide = lax.broadcasted_iota(jnp.int32, (16, 128), 1)
    even = ((wide // 8) % 2) == 0
    quarter = wide // 32
    for g in range(BLK // 4):
        pieces = [[msg_ref[4 * g + i, :, pl.ds(128 * h, 128)].astype(F32) for h in range(2)] for i in range(4)]
        for c in range(COMPS):
            total = None
            for i in range(4):
                piece = pieces[i][c // 4]
                shift = (32 * (i - c)) % 128
                moved = pltpu.roll(piece, shift, 1) if shift else piece
                total = moved if total is None else jnp.where(quarter == i, moved, total)
            left[16 * c : 16 * c + 16, pl.ds(128 * g, 128)] = jnp.where(even, total, 0.0).astype(BF16)
            left[96 + 16 * c : 112 + 16 * c, pl.ds(128 * g, 128)] = jnp.where(even, 0.0, total).astype(BF16)

    for u in range(KH // 256):
        cols = pl.ds(256 * u, 256)
        field = jnp.dot(left[...], wave[:, cols], preferred_element_type=F32)
        low, high = vis[:, cols], vis[:, pl.ds(KH + 256 * u, 256)]
        for c in range(COMPS):
            e, o = field[16 * c : 16 * c + 16], field[96 + 16 * c : 112 + 16 * c]
            first, second = low * (e + o), high * (e - o)
            pm[16 * c : 16 * c + 16, cols] = (first + second).astype(BF16)
            pm[96 + 16 * c : 112 + 16 * c, cols] = (first - second).astype(BF16)

    def back(b, _):
        rows = pl.ds(pl.multiple_of(b * 256, 256), 256)
        both = lax.dot_general(pm[...], wave[rows, :], NT, preferred_element_type=F32)
        lanes = lax.broadcasted_iota(jnp.int32, (96, 256), 1)
        pick = ((lanes // 8) % 2) == 0
        spect[:, rows] = jnp.where(pick, both[:96], both[96:]) * (2.0 * math.pi / POINTS)
        return 0

    lax.fori_loop(0, POINTS // 256, back, 0)

    for g in range(BLK // 4):
        vals = [spect[16 * c : 16 * c + 16, pl.ds(128 * g, 128)] for c in range(COMPS)]
        for i in range(4):
            for h in range(2):
                total = None
                for c in range(4 * h, min(4 * h + 4, COMPS)):
                    shift = (32 * (c - i)) % 128
                    moved = pltpu.roll(vals[c], shift, 1) if shift else vals[c]
                    total = moved if total is None else jnp.where(quarter == c % 4, moved, total)
                out_ref[4 * g + i, :, pl.ds(128 * h, 128)] = total.astype(BF16)


def run_longitude(flip, me, shift, vis, msg):
    whole = pl.BlockSpec(memory_space=pltpu.VMEM)
    return pl.pallas_call(
        longitude_kernel,
        in_specs=[pl.BlockSpec(memory_space=pltpu.SMEM), whole, whole, whole, whole],
        out_specs=whole,
        out_shape=jax.ShapeDtypeStruct((BLK, CYC, 256), BF16),
        scratch_shapes=[
            pltpu.VMEM((POINTS, KH), BF16),
            pltpu.VMEM((192, POINTS), BF16),
            pltpu.VMEM((192, KH), BF16),
            pltpu.VMEM((96, POINTS), F32),
            pltpu.VMEM((CYC, POINTS), F32),
        ],
        name="longitude",
    )(flip, me, shift, vis, msg)


def analysis_kernel(ord_ref, rad_ref, lat_ref, tab_ref, msg_ref, out_ref, sum_ref, side):
    q = pl.program_id(0)

    @pl.when(q == 0)
    def _():
        for t in range(TILES):
            w = lat_ref[3:4, pl.ds(128 * t, 128)]
            for h in range(2):
                lanes = pl.ds(128 * h, 128)
                north = jnp.concatenate([msg_ref[8 * t + b, :, lanes].astype(F32) for b in range(8)], axis=0)
                south = jnp.concatenate([msg_ref[BLK - 1 - 8 * t - b, :, lanes].astype(F32) for b in range(8)], axis=0)
                side[t, 0, pl.ds(128 * h, 128), :] = (north + south).T * w
                side[t, 1, pl.ds(128 * h, 128), :] = (north - south).T * w

    par, p = q // 8, q % 8
    slot = 2 * p + ((ord_ref[2 * p] + par) & 1)
    order = ord_ref[slot]
    left = jnp.concatenate(
        [
            jnp.concatenate([side[t, half, pl.ds(q, 16, stride=16), :] for t in range(TILES)], axis=1)
            for half in range(2)
        ],
        axis=0,
    ).astype(BF16)
    both = lax.dot_general(left, tab_ref[0], NT, preferred_element_type=F32)
    deg = lax.broadcasted_iota(jnp.int32, (16, DEG), 1)
    coef = jnp.where(((deg + order) & 1) == 0, both[:16], both[16:])
    scaled = coef * rad_ref[0]
    for c in range(COMPS):
        out_ref[c, slot] = coef[2 * c : 2 * c + 2].astype(BF16)
        sum_ref[c, slot] = scaled[2 * c : 2 * c + 2].astype(BF16)


def run_analysis(my_orders, rad, lat, tab, msg):
    full = lambda shape: pl.BlockSpec(shape, lambda i: (0,) * len(shape))
    shape = (COMPS, ORDERS, PARTS, DEG)
    return pl.pallas_call(
        analysis_kernel,
        grid=(ORDERS,),
        in_specs=[
            pl.BlockSpec(memory_space=pltpu.SMEM),
            pl.BlockSpec(memory_space=pltpu.SMEM),
            full((8, HALF)),
            pl.BlockSpec((1, DEG, HALF), lambda i: (i, 0, 0)),
            full((BLK, CYC, 256)),
        ],
        out_specs=[full(shape), full(shape)],
        out_shape=[jax.ShapeDtypeStruct(shape, BF16)] * 2,
        scratch_shapes=[pltpu.VMEM((TILES, 2, 256, 128), F32)],
        name="analysis",
    )(my_orders, rad, lat, tab, msg)


def order_columns(order_map, index):
    pairs = order_map.reshape(-1, 2)
    evens = jnp.where(pairs[:, 0] % 2 == 0, pairs[:, 0], pairs[:, 1]).astype(F32)
    me = jnp.broadcast_to(evens.reshape(BLK, 8, 1), (BLK, 8, 128))
    mine = lax.dynamic_slice_in_dim(evens, index * 8, 8)
    mb = jnp.broadcast_to(jnp.stack([mine, (DEG - 1.0) - mine])[:, :, None], (2, 8, 128))
    return me, mb


def shift_table():
    k = np.arange(KH, dtype=np.float64)
    ang = 2.0 * np.pi * k / POINTS
    sign = 1.0 - 2.0 * (k % 2)
    return np.stack([sign * np.cos(ang), sign * np.sin(ang)]).astype(np.float32)


def shards(strain_spec, order_map, viscosity, radial_weight):
    index = lax.axis_index("blk")
    lat, g = latitude_constants()
    lat, g = jnp.asarray(lat), jnp.asarray(g)
    my_orders = lax.dynamic_slice_in_dim(order_map, index * ORDERS, ORDERS)
    me, mb = order_columns(order_map, index)
    tab, msg = run_legendre(my_orders, mb, lat, g, strain_spec.reshape(COMPS, ORDERS, PARTS, DEG))
    msg = lax.all_to_all(msg, "blk", split_axis=0, concat_axis=0, tiled=True)
    flip = (index >= BLK // 2).astype(jnp.int32).reshape(1)
    msg = run_longitude(flip, me, jnp.asarray(shift_table()), viscosity.reshape(CYC, POINTS), msg)
    msg = lax.all_to_all(msg, "blk", split_axis=0, concat_axis=0, tiled=True)
    spec, part = run_analysis(my_orders, radial_weight, lat, tab, msg)
    summed = lax.psum_scatter(part, "shell", scatter_dimension=3, tiled=True)
    return spec.reshape(strain_spec.shape), summed.astype(F32)


def solution(mesh):
    return jax.shard_map(
        shards,
        mesh=mesh,
        in_specs=(P(None, "shell", "blk", None, None), P(), P("shell", "blk", None), P("shell")),
        out_specs=(P(None, "shell", "blk", None, None), P(None, "blk", None, "shell")),
        check_vma=False,
    )
```

```python
import functools
import math

import jax
import jax.numpy as jnp
import numpy as np
from jax import lax
from jax.experimental import pallas as pl
from jax.experimental.pallas import tpu as pltpu
from jax.sharding import PartitionSpec as P

F32 = jnp.float32
BF16 = jnp.bfloat16
COMPS = 6
PARTS = 2
ORDERS = 16
DEG = 1024
HALF = 512
BLK = 64
SHELLS = 4
CYC = 16
POINTS = 2048
KH = POINTS // 2
LB = 256
LSTRIDE = LB + 1
TILES = HALF // 128
BIG = 2.0**40
SMALL = 2.0**-40
NT = (((1,), (1,)), ((), ()))
MESH = pl.DeviceIdType.MESH


def latitude_constants():
    j = np.arange(HALF, dtype=np.float64)
    theta = np.pi * (2.0 * j + 1.0) / (4.0 * HALF)
    x = np.cos(theta)
    logsin = np.log2(np.sin(theta))
    hi = np.round(logsin * 512.0) / 512.0
    lo = logsin - hi
    k = np.arange(1, HALF + 1, dtype=np.float64)
    phase = np.outer(k, 2.0 * j + 1.0) % (4.0 * HALF)
    series = np.sum(np.cos(phase * np.pi / (2.0 * HALF)) / (4.0 * k * k - 1.0)[:, None], axis=0)
    weight = (2.0 / (2.0 * HALF)) * (1.0 - 2.0 * series)
    m = np.arange(DEG, dtype=np.float64)
    fac = np.concatenate([[0.0], np.cumsum(np.log2(1.0 - 0.5 / np.arange(1, DEG)))])
    g = 0.5 * np.log2((2.0 * m + 1.0) / (4.0 * np.pi)) + 0.5 * fac
    lat = np.stack([x, hi, lo, weight]).astype(np.float32)
    return np.concatenate([lat, np.zeros((4, HALF), np.float32)]), g.astype(np.float32)[None]


def legendre_kernel(ord_ref, mb_ref, lat_ref, g_ref, spec_ref, tab_ref, msg_ref, ca, cab, prev, cur, ini, expo, ft, acc, lhs, ns):
    step = pl.program_id(0)

    @pl.when(step == 0)
    def _():
        lane = lax.broadcasted_iota(jnp.int32, (8, 128), 1).astype(F32)
        glane = lax.broadcasted_iota(jnp.int32, (8, DEG), 1).astype(F32)
        for par in range(2):
            m = mb_ref[par]
            for b in range(DEG // 128):
                l = lane + float(128 * b)
                up = l > m
                den = jnp.where(up, (l - m) * (l + m), 1.0)
                a2 = (4.0 * l * l - 1.0) / den
                a = jnp.where(up, jnp.sqrt(jnp.where(up, a2, 1.0)), 0.0)
                below = l - 1.0
                top = jnp.where(below > m, (below - m) * (below + m), 0.0)
                b2 = top / jnp.maximum(4.0 * below * below - 1.0, 1.0)
                ca[b, par] = a
                cab[b, par] = a * jnp.sqrt(b2)
            gm = jnp.sum(jnp.where(glane == m[:, :1], g_ref[...], 0.0), axis=1, keepdims=True)
            for t in range(TILES):
                cols = pl.ds(128 * t, 128)
                mh = m * lat_ref[1:2, cols]
                whole = jnp.floor(mh)
                frac = (mh - whole) + m * lat_ref[2:3, cols] + gm
                ini[par, t] = jnp.exp(frac * math.log(2.0))
                expo[par, t] = whole
                prev[par, t] = jnp.zeros((8, 128), F32)
                cur[par, t] = jnp.zeros((8, 128), F32)

        deg = lax.broadcasted_iota(jnp.int32, (16, DEG), 1)

        def place(q, _):
            par, p = q // 8, q % 8
            slot = 2 * p + ((ord_ref[2 * p] + par) & 1)
            order = ord_ref[slot]
            rows = [spec_ref[c, slot].astype(F32) for c in range(COMPS)]
            rows.append(jnp.zeros((4, DEG), F32))
            data = jnp.concatenate(rows, axis=0) * jnp.where(order == 0, 1.0, 2.0)
            even = ((deg + order) & 1) == 0
            lhs[q, 0:16] = jnp.where(even, data, 0.0).astype(BF16)
            lhs[q, 16:32] = jnp.where(even, 0.0, data).astype(BF16)
            acc[q] = jnp.zeros((32, HALF), F32)
            return 0

        lax.fori_loop(0, ORDERS, place, 0)

    def eight(sub, _):
        block = step * (LB // 128) + sub // 16
        shift = (128 - 8 * (sub % 16)) % 128
        base = step * LB + sub * 8
        av = [pltpu.roll(ca[block, par], shift, 1) for par in range(2)]
        abv = [pltpu.roll(cab[block, par], shift, 1) for par in range(2)]
        xs = [jnp.broadcast_to(lat_ref[0:1, pl.ds(128 * t, 128)], (8, 128)) for t in range(TILES)]
        for par in range(2):
            m = mb_ref[par]
            state = []
            for t in range(TILES):
                e = expo[par, t]
                c, p = cur[par, t], prev[par, t]
                big = jnp.abs(c) > BIG
                f = jnp.where(big, SMALL, 1.0)
                e = jnp.where(big, e + 40.0, e)
                expo[par, t] = e
                scale = jnp.where(e < -126.0, 0.0, jnp.exp(jnp.maximum(e, -126.0) * math.log(2.0)))
                state.append((p * f, c * f, scale, ini[par, t]))
            for r in range(8):
                a = jnp.broadcast_to(av[par][:, r : r + 1], (8, 128))
                ab = jnp.broadcast_to(abv[par][:, r : r + 1], (8, 128))
                hit = m == (base + r).astype(F32)
                for t in range(TILES):
                    p, c, scale, start = state[t]
                    new = (a * xs[t]) * c - ab * p
                    new = jnp.where(hit, start, new)
                    state[t] = (c, new, scale, start)
                    ft[t, pl.ds(par * 8 * LSTRIDE + sub * 8 + r, 8, stride=LSTRIDE), :] = new * scale
            for t in range(TILES):
                prev[par, t] = state[t][0]
                cur[par, t] = state[t][1]
        return 0

    lax.fori_loop(0, LB // 8, eight, 0)

    for q in range(ORDERS):
        table = jnp.concatenate([ft[t, q * LSTRIDE : q * LSTRIDE + LB, :] for t in range(TILES)], axis=1).astype(BF16)
        tab_ref[q] = table
        left = lhs[q, :, pl.ds(pl.multiple_of(step * LB, LB), LB)]
        acc[q] += jnp.dot(left, table, preferred_element_type=F32)

    @pl.when(step == pl.num_programs(0) - 1)
    def _():
        def spread(q, _):
            sym, anti = acc[q, 0:16], acc[q, 16:32]
            for t in range(TILES):
                cols = slice(128 * t, 128 * t + 128)
                ns[t, pl.ds(q, 16, stride=16), :] = sym[:, cols] + anti[:, cols]
                ns[TILES + t, pl.ds(q, 16, stride=16), :] = sym[:, cols] - anti[:, cols]
            return 0

        lax.fori_loop(0, ORDERS, spread, 0)
        for t in range(2 * TILES):
            flipped = jnp.concatenate([ns[t, 0:128].T, ns[t, 128:256].T], axis=1).astype(BF16)
            for b in range(8):
                d = (t % TILES) * 8 + b
                dest = d if t < TILES else BLK - 1 - d
                msg_ref[dest] = flipped[16 * b : 16 * b + 16]


def run_legendre(my_orders, mb, lat, g, spec):
    full = lambda shape: pl.BlockSpec(shape, lambda i: (0,) * len(shape))
    return pl.pallas_call(
        legendre_kernel,
        grid=(DEG // LB,),
        in_specs=[
            pl.BlockSpec(memory_space=pltpu.SMEM),
            full((2, 8, 128)),
            full((8, HALF)),
            full((1, DEG)),
            full((COMPS, ORDERS, PARTS, DEG)),
        ],
        out_specs=[
            pl.BlockSpec((ORDERS, LB, HALF), lambda i: (0, i, 0)),
            full((BLK, CYC, 256)),
        ],
        out_shape=[
            jax.ShapeDtypeStruct((ORDERS, DEG, HALF), BF16),
            jax.ShapeDtypeStruct((BLK, CYC, 256), BF16),
        ],
        scratch_shapes=[
            pltpu.VMEM((DEG // 128, 2, 8, 128), F32),
            pltpu.VMEM((DEG // 128, 2, 8, 128), F32),
            pltpu.VMEM((2, TILES, 8, 128), F32),
            pltpu.VMEM((2, TILES, 8, 128), F32),
            pltpu.VMEM((2, TILES, 8, 128), F32),
            pltpu.VMEM((2, TILES, 8, 128), F32),
            pltpu.VMEM((TILES, ORDERS * LSTRIDE + 8, 128), F32),
            pltpu.VMEM((ORDERS, 32, HALF), F32),
            pltpu.VMEM((ORDERS, 32, DEG), BF16),
            pltpu.VMEM((2 * TILES, 256, 128), F32),
        ],
        name="legendre",
    )(my_orders, mb, lat, g, spec)


def turn(phase):
    t = phase * (1.0 / KH) - 1.0
    z = t * t
    c = jnp.full_like(z, 0.0)
    s = jnp.full_like(z, 0.0)
    for i in range(8, -1, -1):
        c = c * z + float((-1) ** (i + 1) * math.pi ** (2 * i) / math.factorial(2 * i))
        s = s * z + float((-1) ** (i + 1) * math.pi ** (2 * i + 1) / math.factorial(2 * i + 1))
    return c, s * t


def wrap(value):
    return value - POINTS * jnp.floor(value * (1.0 / POINTS))


def longitude_kernel(me_ref, shift_ref, vis_ref, msg_ref, out_ref, wave, left, pm, spect, vis, got, give, sems):
    here = lax.axis_index("blk")
    barrier = pltpu.get_barrier_semaphore()

    def greet(i, _):
        pl.semaphore_signal(barrier, inc=1, device_id={"blk": lax.rem(here + i, BLK)}, device_id_type=MESH)
        return 0

    lax.fori_loop(1, BLK, greet, 0)
    pl.semaphore_wait(barrier, BLK - 1)

    def first_copy(peer, mine):
        return pltpu.make_async_remote_copy(
            src_ref=msg_ref.at[peer], dst_ref=got.at[mine], send_sem=sems.at[0], recv_sem=sems.at[1],
            device_id={"blk": peer}, device_id_type=MESH,
        )

    def send_first(i, _):
        first_copy(lax.rem(here + i, BLK), here).start()
        return 0

    lax.fori_loop(1, BLK, send_first, 0)
    own = pltpu.make_async_copy(msg_ref.at[here], got.at[here], sems.at[4])
    own.start()

    lane = lax.broadcasted_iota(jnp.int32, (8, 128), 1).astype(F32)
    sc, ss = [], []
    for u in range(KH // 128):
        sc.append(jnp.broadcast_to(shift_ref[0:1, pl.ds(128 * u, 128)], (8, 128)))
        ss.append(jnp.broadcast_to(shift_ref[1:2, pl.ds(128 * u, 128)], (8, 128)))

    def make(src, _):
        m = me_ref[src]
        c, s = turn(wrap(m * lane))
        gc, gs = turn(wrap(m * 128.0))
        for u in range(KH // 128):
            oc = sc[u] * c - ss[u] * s
            os = -(ss[u] * c + sc[u] * s)
            rows = pl.ds(pl.multiple_of(src * 32, 32), 32)
            wave[rows, pl.ds(128 * u, 128)] = jnp.concatenate([c, oc, -s, -os], axis=0).astype(BF16)
            c, s = c * gc - s * gs, s * gc + c * gs
        return 0

    lax.fori_loop(0, BLK, make, 0)

    for j in range(CYC):
        row = jnp.where(here >= BLK // 2, CYC - 1 - j, j)
        vis[j : j + 1, :] = vis_ref[pl.ds(row, 1), :]

    own.wait()
    pltpu.make_async_remote_copy(
        src_ref=msg_ref.at[0 : BLK - 1], dst_ref=got.at[0 : BLK - 1], send_sem=sems.at[0], recv_sem=sems.at[1],
        device_id={"blk": here}, device_id_type=MESH,
    ).wait()

    wide = lax.broadcasted_iota(jnp.int32, (16, 128), 1)
    even = ((wide // 8) % 2) == 0
    quarter = wide // 32
    for g in range(BLK // 4):
        pieces = [[got[4 * g + i, :, pl.ds(128 * h, 128)].astype(F32) for h in range(2)] for i in range(4)]
        for c in range(COMPS):
            total = None
            for i in range(4):
                piece = pieces[i][c // 4]
                shift = (32 * (i - c)) % 128
                moved = pltpu.roll(piece, shift, 1) if shift else piece
                total = moved if total is None else jnp.where(quarter == i, moved, total)
            left[16 * c : 16 * c + 16, pl.ds(128 * g, 128)] = jnp.where(even, total, 0.0).astype(BF16)
            left[96 + 16 * c : 112 + 16 * c, pl.ds(128 * g, 128)] = jnp.where(even, 0.0, total).astype(BF16)

    for u in range(KH // 256):
        cols = pl.ds(256 * u, 256)
        field = jnp.dot(left[...], wave[:, cols], preferred_element_type=F32)
        low, high = vis[:, cols], vis[:, pl.ds(KH + 256 * u, 256)]
        for c in range(COMPS):
            e, o = field[16 * c : 16 * c + 16], field[96 + 16 * c : 112 + 16 * c]
            first, second = low * (e + o), high * (e - o)
            pm[16 * c : 16 * c + 16, cols] = (first + second).astype(BF16)
            pm[96 + 16 * c : 112 + 16 * c, cols] = (first - second).astype(BF16)

    def back(b, _):
        rows = pl.ds(pl.multiple_of(b * 256, 256), 256)
        both = lax.dot_general(pm[...], wave[rows, :], NT, preferred_element_type=F32)
        lanes = lax.broadcasted_iota(jnp.int32, (96, 256), 1)
        pick = ((lanes // 8) % 2) == 0
        spect[:, rows] = jnp.where(pick, both[:96], both[96:]) * (2.0 * math.pi / POINTS)
        return 0

    lax.fori_loop(0, POINTS // 256, back, 0)

    def pack(g, _):
        cols = pl.ds(pl.multiple_of(g * 128, 128), 128)
        vals = [spect[16 * c : 16 * c + 16, cols] for c in range(COMPS)]
        for i in range(4):
            for h in range(2):
                total = None
                for c in range(4 * h, min(4 * h + 4, COMPS)):
                    shift = (32 * (c - i)) % 128
                    moved = pltpu.roll(vals[c], shift, 1) if shift else vals[c]
                    total = moved if total is None else jnp.where(quarter == c % 4, moved, total)
                give[4 * g + i, :, pl.ds(128 * h, 128)] = total.astype(BF16)
        return 0

    lax.fori_loop(0, BLK // 4, pack, 0)

    def send_second(i, _):
        peer = lax.rem(here + i, BLK)
        pltpu.make_async_remote_copy(
            src_ref=give.at[peer], dst_ref=out_ref.at[here], send_sem=sems.at[2], recv_sem=sems.at[3],
            device_id={"blk": peer}, device_id_type=MESH,
        ).start()
        return 0

    lax.fori_loop(1, BLK, send_second, 0)
    own = pltpu.make_async_copy(give.at[here], out_ref.at[here], sems.at[4])
    own.start()
    own.wait()
    pltpu.make_async_remote_copy(
        src_ref=give.at[0 : BLK - 1], dst_ref=out_ref.at[0 : BLK - 1], send_sem=sems.at[2], recv_sem=sems.at[3],
        device_id={"blk": here}, device_id_type=MESH,
    ).wait()


def run_longitude(me, shift, vis, msg):
    whole = pl.BlockSpec(memory_space=pltpu.VMEM)
    return pl.pallas_call(
        longitude_kernel,
        in_specs=[whole] * 4,
        out_specs=pl.BlockSpec(memory_space=pl.ANY),
        out_shape=jax.ShapeDtypeStruct((BLK, CYC, 256), BF16),
        scratch_shapes=[
            pltpu.VMEM((POINTS, KH), BF16),
            pltpu.VMEM((192, POINTS), BF16),
            pltpu.VMEM((192, KH), BF16),
            pltpu.VMEM((96, POINTS), F32),
            pltpu.VMEM((CYC, POINTS), F32),
            pltpu.VMEM((BLK, CYC, 256), BF16),
            pltpu.VMEM((BLK, CYC, 256), BF16),
            pltpu.SemaphoreType.DMA((5,)),
        ],
        compiler_params=pltpu.CompilerParams(collective_id=0, has_side_effects=True),
        name="longitude",
    )(me, shift, vis, msg)


def gather_kernel(part_ref, out_ref, got, sems):
    here = lax.axis_index("shell")
    barrier = pltpu.get_barrier_semaphore()
    for i in range(1, SHELLS):
        pl.semaphore_signal(barrier, inc=1, device_id={"shell": lax.rem(here + i, SHELLS)}, device_id_type=MESH)
    pl.semaphore_wait(barrier, SHELLS - 1)
    copies = []
    for i in range(1, SHELLS):
        peer = lax.rem(here + i, SHELLS)
        copy = pltpu.make_async_remote_copy(
            src_ref=part_ref.at[peer], dst_ref=got.at[i - 1], send_sem=sems.at[0, i - 1], recv_sem=sems.at[1, i - 1],
            device_id={"shell": peer}, device_id_type=MESH,
        )
        copy.start()
        copies.append(copy)
    for copy in copies:
        copy.wait()
    for c in range(COMPS):
        total = part_ref[here, c].astype(F32)
        for i in range(SHELLS - 1):
            total = total + got[i, c].astype(F32)
        out_ref[c] = total


def run_gather(part):
    whole = pl.BlockSpec(memory_space=pltpu.VMEM)
    shape = (COMPS, ORDERS, PARTS, DEG // SHELLS)
    return pl.pallas_call(
        gather_kernel,
        in_specs=[whole],
        out_specs=whole,
        out_shape=jax.ShapeDtypeStruct(shape, F32),
        scratch_shapes=[pltpu.VMEM((SHELLS - 1,) + shape, BF16), pltpu.SemaphoreType.DMA((2, SHELLS - 1))],
        compiler_params=pltpu.CompilerParams(collective_id=1, has_side_effects=True),
        name="gather",
    )(part)


def analysis_kernel(ord_ref, rad_ref, lat_ref, tab_ref, msg_ref, out_ref, sum_ref, side):
    q = pl.program_id(0)

    @pl.when(q == 0)
    def _():
        for t in range(TILES):
            w = lat_ref[3:4, pl.ds(128 * t, 128)]
            for h in range(2):
                lanes = pl.ds(128 * h, 128)
                north = jnp.concatenate([msg_ref[8 * t + b, :, lanes].astype(F32) for b in range(8)], axis=0)
                south = jnp.concatenate([msg_ref[BLK - 1 - 8 * t - b, :, lanes].astype(F32) for b in range(8)], axis=0)
                side[t, 0, pl.ds(128 * h, 128), :] = (north + south).T * w
                side[t, 1, pl.ds(128 * h, 128), :] = (north - south).T * w

    par, p = q // 8, q % 8
    slot = 2 * p + ((ord_ref[2 * p] + par) & 1)
    order = ord_ref[slot]
    left = jnp.concatenate(
        [
            jnp.concatenate([side[t, half, pl.ds(q, 16, stride=16), :] for t in range(TILES)], axis=1)
            for half in range(2)
        ],
        axis=0,
    ).astype(BF16)
    both = lax.dot_general(left, tab_ref[0], NT, preferred_element_type=F32)
    deg = lax.broadcasted_iota(jnp.int32, (16, DEG), 1)
    coef = jnp.where(((deg + order) & 1) == 0, both[:16], both[16:])
    scaled = coef * rad_ref[0]
    for c in range(COMPS):
        out_ref[c, slot] = coef[2 * c : 2 * c + 2].astype(BF16)
        for i in range(SHELLS):
            share = DEG // SHELLS
            sum_ref[i, c, slot] = scaled[2 * c : 2 * c + 2, i * share : (i + 1) * share].astype(BF16)


def run_analysis(my_orders, rad, lat, tab, msg):
    full = lambda shape: pl.BlockSpec(shape, lambda i: (0,) * len(shape))
    shape = (COMPS, ORDERS, PARTS, DEG)
    split = (SHELLS, COMPS, ORDERS, PARTS, DEG // SHELLS)
    return pl.pallas_call(
        analysis_kernel,
        grid=(ORDERS,),
        in_specs=[
            pl.BlockSpec(memory_space=pltpu.SMEM),
            pl.BlockSpec(memory_space=pltpu.SMEM),
            full((8, HALF)),
            pl.BlockSpec((1, DEG, HALF), lambda i: (i, 0, 0)),
            full((BLK, CYC, 256)),
        ],
        out_specs=[full(shape), full(split)],
        out_shape=[jax.ShapeDtypeStruct(shape, BF16), jax.ShapeDtypeStruct(split, BF16)],
        scratch_shapes=[pltpu.VMEM((TILES, 2, 256, 128), F32)],
        name="analysis",
    )(my_orders, rad, lat, tab, msg)


def order_columns(order_map, index):
    pairs = order_map.reshape(-1, 2)
    evens = jnp.where(pairs[:, 0] % 2 == 0, pairs[:, 0], pairs[:, 1]).astype(F32)
    me = jnp.broadcast_to(evens.reshape(BLK, 8, 1), (BLK, 8, 128))
    mine = lax.dynamic_slice_in_dim(evens, index * 8, 8)
    mb = jnp.broadcast_to(jnp.stack([mine, (DEG - 1.0) - mine])[:, :, None], (2, 8, 128))
    return me, mb


def shift_table():
    k = np.arange(KH, dtype=np.float64)
    ang = 2.0 * np.pi * k / POINTS
    sign = 1.0 - 2.0 * (k % 2)
    return np.stack([sign * np.cos(ang), sign * np.sin(ang)]).astype(np.float32)


def shards(strain_spec, order_map, viscosity, radial_weight):
    index = lax.axis_index("blk")
    lat, g = latitude_constants()
    lat, g = jnp.asarray(lat), jnp.asarray(g)
    my_orders = lax.dynamic_slice_in_dim(order_map, index * ORDERS, ORDERS)
    me, mb = order_columns(order_map, index)
    tab, msg = run_legendre(my_orders, mb, lat, g, strain_spec.reshape(COMPS, ORDERS, PARTS, DEG))
    msg = run_longitude(me, jnp.asarray(shift_table()), viscosity.reshape(CYC, POINTS), msg)
    spec, part = run_analysis(my_orders, radial_weight, lat, tab, msg)
    return spec.reshape(strain_spec.shape), run_gather(part)


def solution(mesh):
    return jax.shard_map(
        shards,
        mesh=mesh,
        in_specs=(P(None, "shell", "blk", None, None), P(), P("shell", "blk", None), P("shell")),
        out_specs=(P(None, "shell", "blk", None, None), P(None, "blk", None, "shell")),
        check_vma=False,
    )
```

```python
import functools
import math

import jax
import jax.numpy as jnp
import numpy as np
from jax import lax
from jax.experimental import pallas as pl
from jax.experimental.pallas import tpu as pltpu
from jax.sharding import PartitionSpec as P

F32 = jnp.float32
BF16 = jnp.bfloat16
COMPS = 6
PARTS = 2
ORDERS = 16
DEG = 1024
HALF = 512
BLK = 64
SHELLS = 4
CYC = 16
POINTS = 2048
KH = POINTS // 2
LB = 256
LSTRIDE = LB + 1
TILES = HALF // 128
PAIRS = 8
STEPS = DEG // LB + 1
TURN = 16
TURNS = LB // TURN
BIG = 2.0**40
SMALL = 2.0**-40
NT = (((1,), (1,)), ((), ()))
MESH = pl.DeviceIdType.MESH


def latitude_constants():
    j = np.arange(HALF, dtype=np.float64)
    theta = np.pi * (2.0 * j + 1.0) / (4.0 * HALF)
    x = np.cos(theta)
    logsin = np.log2(np.sin(theta))
    hi = np.round(logsin * 512.0) / 512.0
    lo = logsin - hi
    k = np.arange(1, HALF + 1, dtype=np.float64)
    phase = np.outer(k, 2.0 * j + 1.0) % (4.0 * HALF)
    series = np.sum(np.cos(phase * np.pi / (2.0 * HALF)) / (4.0 * k * k - 1.0)[:, None], axis=0)
    weight = (2.0 / (2.0 * HALF)) * (1.0 - 2.0 * series)
    m = np.arange(DEG, dtype=np.float64)
    fac = np.concatenate([[0.0], np.cumsum(np.log2(1.0 - 0.5 / np.arange(1, DEG)))])
    g = 0.5 * np.log2((2.0 * m + 1.0) / (4.0 * np.pi)) + 0.5 * fac
    lat = np.stack([x, hi, lo, weight]).astype(np.float32)
    return np.concatenate([lat, np.zeros((4, HALF), np.float32)]), g.astype(np.float32)[None]


def power_of(e):
    return jnp.where(e < -126.0, 0.0, jnp.exp(jnp.maximum(e, -126.0) * math.log(2.0)))


def legendre_kernel(ord_ref, lat_ref, g_ref, spec_ref, tab_ref, tail_ref, msg_ref, ca, cab, prev, cur, expo, ini, ini2, expo2, scale2, mark, bca, bcb, ft, acc, lhs, lt, tailb, ns, flag):
    step = pl.program_id(0)
    base = lax.axis_index("blk") * ORDERS
    sub8 = lax.broadcasted_iota(jnp.int32, (8, 128), 0)

    @pl.when(step == 0)
    def _():
        def clear(i, _):
            flag[i] = 0
            return 0

        lax.fori_loop(0, STEPS * PAIRS, clear, 0)
        flag[0] = 1
        even = jnp.zeros((8, 128), jnp.int32)
        for p in range(PAIRS):
            first = ord_ref[base + 2 * p]
            e = jnp.where((first & 1) == 0, first, DEG - 1 - first)
            even = jnp.where(sub8 == p, e, even)
            flag[(DEG - e) // (2 * TURN)] = 1
        ma = even.astype(F32)
        mb = (DEG - 1.0) - ma
        mark[...] = mb + 1.0
        lane = lax.broadcasted_iota(jnp.int32, (8, 128), 1).astype(F32)
        for b in range(STEPS * LB // 128 + 1):
            t = lane + float(128 * b)
            second = t > mb
            m = jnp.where(second, mb, ma)
            l = jnp.where(second, t - 1.0, t + ma)
            up = (l > m) & (t < DEG + 0.5)
            a2 = (4.0 * l * l - 1.0) / jnp.where(up, (l - m) * (l + m), 1.0)
            a = jnp.where(up, jnp.sqrt(jnp.where(up, a2, 1.0)), 0.0)
            below = l - 1.0
            top = jnp.where(below > m, (below - m) * (below + m), 0.0)
            ab = a * jnp.sqrt(top / jnp.maximum(4.0 * below * below - 1.0, 1.0))
            for k in range(128 // TURN):
                ca[b * (128 // TURN) + k] = pltpu.roll(a, (128 - TURN * k) % 128, 1)
                cab[b * (128 // TURN) + k] = pltpu.roll(ab, (128 - TURN * k) % 128, 1)
        glane = lax.broadcasted_iota(jnp.int32, (8, DEG), 1).astype(F32)
        for m, first, power in ((ma, ini, expo), (mb, ini2, expo2)):
            gm = jnp.sum(jnp.where(glane == m[:, :1], g_ref[...], 0.0), axis=1, keepdims=True)
            for t in range(TILES):
                cols = pl.ds(128 * t, 128)
                mh = m * lat_ref[1:2, cols]
                whole = jnp.floor(mh)
                first[t] = jnp.exp(((mh - whole) + m * lat_ref[2:3, cols] + gm) * math.log(2.0))
                power[t] = whole
        for r in range(TURN):
            bca[r, 0] = jnp.broadcast_to(ca[0][:, r : r + 1], (8, 128))
            bca[r, 1] = jnp.broadcast_to(cab[0][:, r : r + 1], (8, 128))
        for t in range(TILES):
            scale2[t] = power_of(expo2[t])
            prev[t] = jnp.zeros((8, 128), F32)
            cur[t] = jnp.zeros((8, 128), F32)

        pos = lax.broadcasted_iota(jnp.int32, (16, DEG), 1)
        pos_even = (pos & 1) == 0
        narrow = lax.broadcasted_iota(jnp.int32, (16, 128), 1)

        def place(p, _):
            first = ord_ref[base + 2 * p]
            odd_first = first & 1
            e = jnp.where(odd_first == 0, first, DEG - 1 - first)
            pads = [jnp.zeros((4, DEG), F32)]
            da = jnp.concatenate([spec_ref[c, 0, 2 * p + odd_first].astype(F32) for c in range(COMPS)] + pads, axis=0)
            db = jnp.concatenate([spec_ref[c, 0, 2 * p + 1 - odd_first].astype(F32) for c in range(COMPS)] + pads, axis=0)
            da = da * jnp.where(e == 0, 1.0, 2.0)
            db = db * 2.0
            last = jnp.broadcast_to(db[:, DEG - 1 : DEG], (16, 128))
            lt[pl.ds(pl.multiple_of(16 * p, 16), 16), :] = jnp.where(narrow == p, last, 0.0).astype(BF16)
            da = pltpu.roll(da, jnp.where(e == 0, 0, DEG - e), 1)
            db = pltpu.roll(db, 1, 1)
            da = jnp.where(pos < DEG - e, da, 0.0)
            db = jnp.where(pos >= DEG - e, db, 0.0)
            lhs[p, 0:16] = jnp.where(pos_even, da, 0.0).astype(BF16)
            lhs[p, 16:32] = jnp.where(pos_even, 0.0, da).astype(BF16)
            lhs[p, 32:48] = jnp.where(pos_even, db, 0.0).astype(BF16)
            lhs[p, 48:64] = jnp.where(pos_even, 0.0, db).astype(BF16)
            return 0

        lax.fori_loop(0, PAIRS, place, 0)

    @pl.when(step == 1)
    def _():
        acc[...] = jnp.zeros_like(acc)

    new_half, old_half = lax.rem(step, 2), lax.rem(step + 1, 2)
    back = jnp.maximum(step - 1, 0)

    def advance(i, starts):
        rows = pl.ds(i * LSTRIDE, LB)
        left = lhs[i, :, pl.ds(pl.multiple_of(back * LB, LB), LB)]
        for half in range(2):
            table = jnp.concatenate([ft[old_half, 2 * half, rows, :], ft[old_half, 2 * half + 1, rows, :]], axis=1).astype(BF16)
            tab_ref[i, :, 256 * half : 256 * half + 256] = table
            acc[i, half] += jnp.dot(left, table, preferred_element_type=F32)

        xs = [jnp.broadcast_to(lat_ref[0:1, pl.ds(128 * t, 128)], (8, 128)) for t in range(TILES)]
        ps, cs, scales = [prev[t] for t in range(TILES)], [cur[t] for t in range(TILES)], [None] * TILES
        es = [expo[t] for t in range(TILES)]
        for k in range(2):
            use, make = (bca, bcb) if k == 0 else (bcb, bca)
            chunk = step * TURNS + 2 * i + k
            av, abv = ca[chunk + 1], cab[chunk + 1]
            for r in range(TURN):
                if r % 8 == 0:
                    for t in range(TILES):
                        big = jnp.abs(cs[t]) > BIG
                        f = jnp.where(big, SMALL, 1.0)
                        es[t] = jnp.where(big, es[t] + 40.0, es[t])
                        scales[t] = power_of(es[t])
                        ps[t], cs[t] = ps[t] * f, cs[t] * f
                make[r, 0] = jnp.broadcast_to(av[:, r : r + 1], (8, 128))
                make[r, 1] = jnp.broadcast_to(abv[:, r : r + 1], (8, 128))
                a, ab = use[r, 0], use[r, 1]
                if starts:
                    now = (chunk * TURN + r).astype(F32)
                    hit = mark[...] == now
                for t in range(TILES):
                    new = (a * xs[t]) * cs[t] - ab * ps[t]
                    if starts:
                        new = jnp.where(hit, ini2[t], new)
                        es[t] = jnp.where(hit, expo2[t], es[t])
                        scales[t] = jnp.where(hit, scale2[t], scales[t])
                        if r == 0 and k == 0:
                            new = jnp.where(jnp.full((8, 128), now) == 0.0, ini[t], new)
                    ps[t], cs[t] = cs[t], new
                    ft[new_half, t, pl.ds(2 * TURN * i + TURN * k + r, 8, stride=LSTRIDE), :] = new * scales[t]
        for t in range(TILES):
            prev[t], cur[t], expo[t] = ps[t], cs[t], es[t]

    def body(i, _):
        starting = flag[step * PAIRS + i] == 1

        @pl.when(starting)
        def _():
            advance(i, True)

        @pl.when(jnp.logical_not(starting))
        def _():
            advance(i, False)

        return 0

    lax.fori_loop(0, PAIRS, body, 0)

    @pl.when(step == STEPS - 1)
    def _():
        tail = jnp.concatenate([ft[new_half, t, pl.ds(0, 8, stride=LSTRIDE), :] for t in range(TILES)], axis=1)
        tailb[...] = jnp.concatenate([tail, jnp.zeros((8, HALF), F32)], axis=0).astype(BF16)
        tail_ref[...] = tailb[...]

        def spread(p, _):
            extra = jnp.dot(lt[pl.ds(pl.multiple_of(16 * p, 16), 16), 0:16], tailb[...], preferred_element_type=F32)
            for t in range(TILES):
                cols = slice(128 * (t % 2), 128 * (t % 2) + 128)
                part = acc[p, t // 2]
                for par in range(2):
                    sym, anti = part[32 * par : 32 * par + 16, cols], part[32 * par + 16 : 32 * par + 32, cols]
                    if par:
                        sym = sym + extra[:, 128 * t : 128 * t + 128]
                    ns[t, pl.ds(par * 8 + p, 16, stride=16), :] = sym + anti
                    ns[TILES + t, pl.ds(par * 8 + p, 16, stride=16), :] = sym - anti
            return 0

        lax.fori_loop(0, PAIRS, spread, 0)
        lane = lax.broadcasted_iota(jnp.int32, (8, 128), 1)
        for t in range(2 * TILES):
            near, far = ns[t, 0:128].T, ns[t, 128:256].T
            moved = pltpu.roll(far, 64, 1)
            for b in range(8):
                d = (t % TILES) * 8 + b
                dest = d if t < TILES else BLK - 1 - d
                msg_ref[dest, 0:16] = near[16 * b : 16 * b + 16].astype(BF16)
                msg_ref[dest, 16:24] = jnp.where(lane < 64, far[16 * b : 16 * b + 8], moved[16 * b + 8 : 16 * b + 16]).astype(BF16)


def run_legendre(order_map, lat, g, spec):
    full = lambda shape: pl.BlockSpec(shape, lambda i: (0,) * len(shape))
    return pl.pallas_call(
        legendre_kernel,
        grid=(STEPS,),
        in_specs=[
            pl.BlockSpec(memory_space=pltpu.SMEM),
            full((8, HALF)),
            full((1, DEG)),
            full((COMPS, 1, ORDERS, PARTS, DEG)),
        ],
        out_specs=[
            pl.BlockSpec((PAIRS, LB, HALF), lambda i: (0, jnp.maximum(i - 1, 0), 0)),
            full((16, HALF)),
            full((BLK, 24, 128)),
        ],
        out_shape=[
            jax.ShapeDtypeStruct((PAIRS, DEG, HALF), BF16),
            jax.ShapeDtypeStruct((16, HALF), BF16),
            jax.ShapeDtypeStruct((BLK, 24, 128), BF16),
        ],
        scratch_shapes=[
            pltpu.VMEM((STEPS * TURNS + 128 // TURN, 8, 128), F32),
            pltpu.VMEM((STEPS * TURNS + 128 // TURN, 8, 128), F32),
            pltpu.VMEM((TILES, 8, 128), F32),
            pltpu.VMEM((TILES, 8, 128), F32),
            pltpu.VMEM((TILES, 8, 128), F32),
            pltpu.VMEM((TILES, 8, 128), F32),
            pltpu.VMEM((TILES, 8, 128), F32),
            pltpu.VMEM((TILES, 8, 128), F32),
            pltpu.VMEM((TILES, 8, 128), F32),
            pltpu.VMEM((8, 128), F32),
            pltpu.VMEM((TURN, 2, 8, 128), F32),
            pltpu.VMEM((TURN, 2, 8, 128), F32),
            pltpu.VMEM((2, TILES, PAIRS * LSTRIDE + 8, 128), F32),
            pltpu.VMEM((PAIRS, 2, 64, 256), F32),
            pltpu.VMEM((PAIRS, 64, DEG), BF16),
            pltpu.VMEM((128, 128), BF16),
            pltpu.VMEM((16, HALF), BF16),
            pltpu.VMEM((2 * TILES, 256, 128), F32),
            pltpu.SMEM((STEPS * PAIRS,), jnp.int32),
        ],
        name="legendre",
    )(order_map, lat, g, spec)


def turn(phase):
    t = phase * (1.0 / KH) - 1.0
    z = t * t
    c = jnp.full_like(z, 0.0)
    s = jnp.full_like(z, 0.0)
    for i in range(8, -1, -1):
        c = c * z + float((-1) ** (i + 1) * math.pi ** (2 * i) / math.factorial(2 * i))
        s = s * z + float((-1) ** (i + 1) * math.pi ** (2 * i + 1) / math.factorial(2 * i + 1))
    return c, s * t


def wrap(value):
    return value - POINTS * jnp.floor(value * (1.0 / POINTS))


def turned(value, quarters):
    return pltpu.roll(value, (32 * quarters) % 128, 1) if quarters % 4 else value


def longitude_kernel(ord_ref, shift_ref, vis_ref, msg_ref, out_ref, wave, left, pm, spect, vis, got, give, sems):
    here = lax.axis_index("blk")
    barrier = pltpu.get_barrier_semaphore()

    def greet(i, _):
        pl.semaphore_signal(barrier, inc=1, device_id={"blk": lax.rem(here + i, BLK)}, device_id_type=MESH)
        return 0

    lax.fori_loop(1, BLK, greet, 0)
    pl.semaphore_wait(barrier, BLK - 1)

    def first_copy(peer, mine):
        return pltpu.make_async_remote_copy(
            src_ref=msg_ref.at[peer], dst_ref=got.at[mine], send_sem=sems.at[0], recv_sem=sems.at[1],
            device_id={"blk": peer}, device_id_type=MESH,
        )

    def send_first(i, _):
        first_copy(lax.rem(here + i, BLK), here).start()
        return 0

    lax.fori_loop(1, BLK, send_first, 0)
    own = pltpu.make_async_copy(msg_ref.at[here], got.at[here], sems.at[4])
    own.start()

    lane = lax.broadcasted_iota(jnp.int32, (8, 128), 1).astype(F32)
    sub8 = lax.broadcasted_iota(jnp.int32, (8, 128), 0)
    sc, ss = [], []
    for u in range(KH // 128):
        sc.append(jnp.broadcast_to(shift_ref[0:1, pl.ds(128 * u, 128)], (8, 128)))
        ss.append(jnp.broadcast_to(shift_ref[1:2, pl.ds(128 * u, 128)], (8, 128)))

    def make(src, _):
        even = jnp.zeros((8, 128), jnp.int32)
        for p in range(PAIRS):
            first = ord_ref[src * ORDERS + 2 * p]
            even = jnp.where(sub8 == p, jnp.where((first & 1) == 0, first, DEG - 1 - first), even)
        m = even.astype(F32)
        c, s = turn(wrap(m * lane))
        gc, gs = turn(wrap(m * 128.0))
        for u in range(KH // 128):
            oc = sc[u] * c - ss[u] * s
            os = -(ss[u] * c + sc[u] * s)
            rows = pl.ds(pl.multiple_of(src * 32, 32), 32)
            wave[rows, pl.ds(128 * u, 128)] = jnp.concatenate([c, oc, -s, -os], axis=0).astype(BF16)
            c, s = c * gc - s * gs, s * gc + c * gs
        return 0

    lax.fori_loop(0, BLK, make, 0)

    for j in range(CYC):
        row = jnp.where(here >= BLK // 2, CYC - 1 - j, j)
        vis[j : j + 1, :] = vis_ref[0, pl.ds(row, 1), :]

    own.wait()
    pltpu.make_async_remote_copy(
        src_ref=msg_ref.at[0 : BLK - 1], dst_ref=got.at[0 : BLK - 1], send_sem=sems.at[0], recv_sem=sems.at[1],
        device_id={"blk": here}, device_id_type=MESH,
    ).wait()

    wide = lax.broadcasted_iota(jnp.int32, (16, 128), 1)
    even = ((wide // 8) % 2) == 0
    quarter = wide // 32
    for g in range(BLK // 4):
        pieces = [(got[4 * g + i, 0:16].astype(F32), got[4 * g + i, 16:24].astype(F32)) for i in range(4)]
        for c in range(COMPS):
            total = None
            for i in range(4):
                near, far = pieces[i]
                moved = turned(near, i - c) if c < 4 else jnp.concatenate([turned(far, i - c), turned(far, i - c - 2)], axis=0)
                total = moved if total is None else jnp.where(quarter == i, moved, total)
            left[16 * c : 16 * c + 16, pl.ds(128 * g, 128)] = jnp.where(even, total, 0.0).astype(BF16)
            left[96 + 16 * c : 112 + 16 * c, pl.ds(128 * g, 128)] = jnp.where(even, 0.0, total).astype(BF16)

    for u in range(KH // 256):
        cols = pl.ds(256 * u, 256)
        field = jnp.dot(left[...], wave[:, cols], preferred_element_type=F32)
        low, high = vis[:, cols], vis[:, pl.ds(KH + 256 * u, 256)]
        for c in range(COMPS):
            e, o = field[16 * c : 16 * c + 16], field[96 + 16 * c : 112 + 16 * c]
            first, second = low * (e + o), high * (e - o)
            pm[16 * c : 16 * c + 16, cols] = (first + second).astype(BF16)
            pm[96 + 16 * c : 112 + 16 * c, cols] = (first - second).astype(BF16)

    def back(b, _):
        rows = pl.ds(pl.multiple_of(b * 256, 256), 256)
        both = lax.dot_general(pm[...], wave[rows, :], NT, preferred_element_type=F32)
        lanes = lax.broadcasted_iota(jnp.int32, (96, 256), 1)
        pick = ((lanes // 8) % 2) == 0
        spect[:, rows] = jnp.where(pick, both[:96], both[96:]) * (2.0 * math.pi / POINTS)
        return 0

    lax.fori_loop(0, POINTS // 256, back, 0)

    def pack(g, _):
        cols = pl.ds(pl.multiple_of(g * 128, 128), 128)
        vals = [spect[16 * c : 16 * c + 16, cols] for c in range(COMPS)]
        for i in range(4):
            near = None
            for c in range(4):
                moved = turned(vals[c], c - i)
                near = moved if near is None else jnp.where(quarter == c, moved, near)
            far = None
            for c in range(4):
                moved = turned(vals[4 + c % 2][8 * (c // 2) : 8 * (c // 2) + 8], c - i)
                far = moved if far is None else jnp.where(quarter[:8] == c, moved, far)
            give[4 * g + i, 0:16] = near.astype(BF16)
            give[4 * g + i, 16:24] = far.astype(BF16)
        return 0

    lax.fori_loop(0, BLK // 4, pack, 0)

    def send_second(i, _):
        peer = lax.rem(here + i, BLK)
        pltpu.make_async_remote_copy(
            src_ref=give.at[peer], dst_ref=out_ref.at[here], send_sem=sems.at[2], recv_sem=sems.at[3],
            device_id={"blk": peer}, device_id_type=MESH,
        ).start()
        return 0

    lax.fori_loop(1, BLK, send_second, 0)
    own = pltpu.make_async_copy(give.at[here], out_ref.at[here], sems.at[4])
    own.start()
    own.wait()
    pltpu.make_async_remote_copy(
        src_ref=give.at[0 : BLK - 1], dst_ref=out_ref.at[0 : BLK - 1], send_sem=sems.at[2], recv_sem=sems.at[3],
        device_id={"blk": here}, device_id_type=MESH,
    ).wait()


def run_longitude(order_map, shift, vis, msg):
    whole = pl.BlockSpec(memory_space=pltpu.VMEM)
    return pl.pallas_call(
        longitude_kernel,
        in_specs=[pl.BlockSpec(memory_space=pltpu.SMEM)] + [whole] * 3,
        out_specs=pl.BlockSpec(memory_space=pl.ANY),
        out_shape=jax.ShapeDtypeStruct((BLK, 24, 128), BF16),
        scratch_shapes=[
            pltpu.VMEM((POINTS, KH), BF16),
            pltpu.VMEM((192, POINTS), BF16),
            pltpu.VMEM((192, KH), BF16),
            pltpu.VMEM((96, POINTS), F32),
            pltpu.VMEM((CYC, POINTS), F32),
            pltpu.VMEM((BLK, 24, 128), BF16),
            pltpu.VMEM((BLK, 24, 128), BF16),
            pltpu.SemaphoreType.DMA((5,)),
        ],
        compiler_params=pltpu.CompilerParams(collective_id=0, has_side_effects=True),
        name="longitude",
    )(order_map, shift, vis, msg)


def gather_kernel(part_ref, out_ref, near, total, give, far, sems):
    here = lax.axis_index("shell")
    layer, core = here // 2, lax.rem(here, 2)
    partner, across = 2 * layer + 1 - core, 2 * (1 - layer) + core
    barrier = pltpu.get_barrier_semaphore()
    for peer in (partner, across):
        pl.semaphore_signal(barrier, inc=1, device_id={"shell": peer}, device_id_type=MESH)
    pl.semaphore_wait(barrier, 2)
    first = []
    for c in range(COMPS):
        for k in range(2):
            share = 2 * (1 - layer if k == 0 else layer) + 1 - core
            copy = pltpu.make_async_remote_copy(
                src_ref=part_ref.at[share, c], dst_ref=near.at[k, c], send_sem=sems.at[0, k, c], recv_sem=sems.at[1, k, c],
                device_id={"shell": partner}, device_id_type=MESH,
            )
            copy.start()
            first.append(copy)
    second = []
    for c in range(COMPS):
        first[2 * c].wait_recv()
        give[c] = (part_ref[across, c].astype(F32) + near[0, c].astype(F32)).astype(BF16)
        copy = pltpu.make_async_remote_copy(
            src_ref=give.at[c], dst_ref=far.at[c], send_sem=sems.at[2, 0, c], recv_sem=sems.at[2, 1, c],
            device_id={"shell": across}, device_id_type=MESH,
        )
        copy.start()
        second.append(copy)
    for c in range(COMPS):
        first[2 * c + 1].wait_recv()
        total[c] = part_ref[here, c].astype(F32) + near[1, c].astype(F32)
    for c in range(COMPS):
        second[c].wait_recv()
        out_ref[c] = total[c] + far[c].astype(F32)
    for copy in first + second:
        copy.wait_send()


def run_gather(part):
    whole = pl.BlockSpec(memory_space=pltpu.VMEM)
    shape = (COMPS, ORDERS, PARTS, DEG // SHELLS)
    return pl.pallas_call(
        gather_kernel,
        in_specs=[whole],
        out_specs=whole,
        out_shape=jax.ShapeDtypeStruct(shape, F32),
        scratch_shapes=[
            pltpu.VMEM((2,) + shape, BF16),
            pltpu.VMEM(shape, F32),
            pltpu.VMEM(shape, BF16),
            pltpu.VMEM(shape, BF16),
            pltpu.SemaphoreType.DMA((3, 2, COMPS)),
        ],
        compiler_params=pltpu.CompilerParams(collective_id=1, has_side_effects=True),
        name="gather",
    )(part)


def analysis_kernel(ord_ref, rad_ref, lat_ref, tail_ref, tab_ref, msg_ref, out_ref, sum_ref, side):
    p = pl.program_id(0)
    base = lax.axis_index("blk") * ORDERS

    @pl.when(p == 0)
    def _():
        def fetch(d):
            near, far = msg_ref[d, 0:16].astype(F32), msg_ref[d, 16:24].astype(F32)
            return near, jnp.concatenate([far, pltpu.roll(far, 64, 1)], axis=0)

        for t in range(TILES):
            w = lat_ref[3:4, pl.ds(128 * t, 128)]
            north = [fetch(8 * t + b) for b in range(8)]
            south = [fetch(BLK - 1 - 8 * t - b) for b in range(8)]
            for h in range(2):
                lanes = pl.ds(128 * h, 128)
                up = jnp.concatenate([v[h] for v in north], axis=0)
                down = jnp.concatenate([v[h] for v in south], axis=0)
                side[t, 0, lanes, :] = (up + down).T * w
                side[t, 1, lanes, :] = (up - down).T * w

    first = ord_ref[base + 2 * p]
    odd_first = first & 1
    e = jnp.where(odd_first == 0, first, DEG - 1 - first)
    left = jnp.concatenate(
        [
            jnp.concatenate([side[t, half, pl.ds(8 * par + p, 16, stride=16), :] for t in range(TILES)], axis=1)
            for par in range(2)
            for half in range(2)
        ],
        axis=0,
    ).astype(BF16)
    both = lax.dot_general(left, tab_ref[0], NT, preferred_element_type=F32)
    final = lax.dot_general(left[32:48], tail_ref[...], NT, preferred_element_type=F32)
    final = jnp.sum(jnp.where(lax.broadcasted_iota(jnp.int32, (16, 16), 1) == p, final, 0.0), axis=1, keepdims=True)
    pos = lax.broadcasted_iota(jnp.int32, (16, DEG), 1)
    pos_even = (pos & 1) == 0
    ca = jnp.where(pos_even, both[0:16], both[16:32])
    cb = jnp.where(pos_even, both[32:48], both[48:64])
    ca = jnp.where(pos >= e, pltpu.roll(ca, e, 1), 0.0)
    cb = jnp.where(pos >= DEG - 1 - e, pltpu.roll(cb, DEG - 1, 1), 0.0)
    cb = jnp.where(pos == DEG - 1, final, cb)
    share = DEG // SHELLS
    for coef, slot in ((ca, 2 * p + odd_first), (cb, 2 * p + 1 - odd_first)):
        scaled = coef * rad_ref[0]
        for c in range(COMPS):
            out_ref[c, 0, slot] = coef[2 * c : 2 * c + 2].astype(BF16)
            for i in range(SHELLS):
                sum_ref[i, c, slot] = scaled[2 * c : 2 * c + 2, i * share : (i + 1) * share].astype(BF16)


def run_analysis(order_map, rad, lat, tail, tab, msg):
    full = lambda shape: pl.BlockSpec(shape, lambda i: (0,) * len(shape))
    shape = (COMPS, 1, ORDERS, PARTS, DEG)
    split = (SHELLS, COMPS, ORDERS, PARTS, DEG // SHELLS)
    return pl.pallas_call(
        analysis_kernel,
        grid=(PAIRS,),
        in_specs=[
            pl.BlockSpec(memory_space=pltpu.SMEM),
            pl.BlockSpec(memory_space=pltpu.SMEM),
            full((8, HALF)),
            full((16, HALF)),
            pl.BlockSpec((1, DEG, HALF), lambda i: (i, 0, 0)),
            full((BLK, 24, 128)),
        ],
        out_specs=[full(shape), full(split)],
        out_shape=[jax.ShapeDtypeStruct(shape, BF16), jax.ShapeDtypeStruct(split, BF16)],
        scratch_shapes=[pltpu.VMEM((TILES, 2, 256, 128), F32)],
        name="analysis",
    )(order_map, rad, lat, tail, tab, msg)


def shift_table():
    k = np.arange(KH, dtype=np.float64)
    ang = 2.0 * np.pi * k / POINTS
    sign = 1.0 - 2.0 * (k % 2)
    return np.stack([sign * np.cos(ang), sign * np.sin(ang)]).astype(np.float32)


def shards(strain_spec, order_map, viscosity, radial_weight):
    lat, g = latitude_constants()
    lat, g = jnp.asarray(lat), jnp.asarray(g)
    tab, tail, msg = run_legendre(order_map, lat, g, strain_spec)
    msg = run_longitude(order_map, jnp.asarray(shift_table()), viscosity, msg)
    spec, part = run_analysis(order_map, radial_weight, lat, tail, tab, msg)
    return spec, run_gather(part)


def solution(mesh):
    return jax.shard_map(
        shards,
        mesh=mesh,
        in_specs=(P(None, "shell", "blk", None, None), P(), P("shell", "blk", None), P("shell")),
        out_specs=(P(None, "shell", "blk", None, None), P(None, "blk", None, "shell")),
        check_vma=False,
    )
```

```python
import math

import jax
import jax.numpy as jnp
import numpy as np
from jax import lax
from jax.experimental import pallas as pl
from jax.experimental.pallas import tpu as pltpu
from jax.sharding import PartitionSpec as P

F32 = jnp.float32
BF16 = jnp.bfloat16
COMPS = 6
PARTS = 2
ORDERS = 16
DEG = 1024
HALF = 512
BLK = 64
SHELLS = 4
CYC = 16
POINTS = 2048
KH = POINTS // 2
LB = 256
LSTRIDE = LB + 1
TILES = HALF // 128
PAIRS = 8
STEPS = DEG // LB + 1
TURN = 16
TURNS = LB // TURN
EARLY = 36
BIG = 2.0**40
SMALL = 2.0**-40
NT = (((1,), (1,)), ((), ()))
MESH = pl.DeviceIdType.MESH


def latitude_constants():
    j = np.arange(HALF, dtype=np.float64)
    theta = np.pi * (2.0 * j + 1.0) / (4.0 * HALF)
    x = np.cos(theta)
    logsin = np.log2(np.sin(theta))
    hi = np.round(logsin * 512.0) / 512.0
    lo = logsin - hi
    k = np.arange(1, HALF + 1, dtype=np.float64)
    phase = np.outer(k, 2.0 * j + 1.0) % (4.0 * HALF)
    series = np.sum(np.cos(phase * np.pi / (2.0 * HALF)) / (4.0 * k * k - 1.0)[:, None], axis=0)
    weight = (2.0 / (2.0 * HALF)) * (1.0 - 2.0 * series)
    m = np.arange(DEG, dtype=np.float64)
    fac = np.concatenate([[0.0], np.cumsum(np.log2(1.0 - 0.5 / np.arange(1, DEG)))])
    g = 0.5 * np.log2((2.0 * m + 1.0) / (4.0 * np.pi)) + 0.5 * fac
    lat = np.stack([x, hi, lo, weight]).astype(np.float32)
    return np.concatenate([lat, np.zeros((4, HALF), np.float32)]), g.astype(np.float32)[None]


def power_of(e):
    return jnp.where(e < -126.0, 0.0, jnp.exp(jnp.maximum(e, -126.0) * math.log(2.0)))


def legendre_kernel(ord_ref, lat_ref, g_ref, spec_ref, tab_ref, tail_ref, msg_ref, ca, cab, prev, cur, expo, ini, ini2, expo2, scale2, mark, bca, bcb, ft, acc, lhs, lt, tailb, ns, flag):
    step = pl.program_id(0)
    base = lax.axis_index("blk") * ORDERS
    sub8 = lax.broadcasted_iota(jnp.int32, (8, 128), 0)

    @pl.when(step == 0)
    def _():
        def clear(i, _):
            flag[i] = 0
            return 0

        lax.fori_loop(0, STEPS * PAIRS, clear, 0)
        flag[0] = 1
        even = jnp.zeros((8, 128), jnp.int32)
        for p in range(PAIRS):
            first = ord_ref[base + 2 * p]
            e = jnp.where((first & 1) == 0, first, DEG - 1 - first)
            even = jnp.where(sub8 == p, e, even)
            flag[(DEG - e) // (2 * TURN)] = 1
        ma = even.astype(F32)
        mb = (DEG - 1.0) - ma
        mark[...] = mb + 1.0
        lane = lax.broadcasted_iota(jnp.int32, (8, 128), 1).astype(F32)
        for b in range(STEPS * LB // 128 + 1):
            t = lane + float(128 * b)
            second = t > mb
            m = jnp.where(second, mb, ma)
            l = jnp.where(second, t - 1.0, t + ma)
            up = (l > m) & (t < DEG + 0.5)
            a2 = (4.0 * l * l - 1.0) / jnp.where(up, (l - m) * (l + m), 1.0)
            a = jnp.where(up, jnp.sqrt(jnp.where(up, a2, 1.0)), 0.0)
            below = l - 1.0
            top = jnp.where(below > m, (below - m) * (below + m), 0.0)
            ab = a * jnp.sqrt(top / jnp.maximum(4.0 * below * below - 1.0, 1.0))
            for k in range(128 // TURN):
                ca[b * (128 // TURN) + k] = pltpu.roll(a, (128 - TURN * k) % 128, 1)
                cab[b * (128 // TURN) + k] = pltpu.roll(ab, (128 - TURN * k) % 128, 1)
        glane = lax.broadcasted_iota(jnp.int32, (8, DEG), 1).astype(F32)
        for m, first, power in ((ma, ini, expo), (mb, ini2, expo2)):
            gm = jnp.sum(jnp.where(glane == m[:, :1], g_ref[...], 0.0), axis=1, keepdims=True)
            for t in range(TILES):
                cols = pl.ds(128 * t, 128)
                mh = m * lat_ref[1:2, cols]
                whole = jnp.floor(mh)
                first[t] = jnp.exp(((mh - whole) + m * lat_ref[2:3, cols] + gm) * math.log(2.0))
                power[t] = whole
        for r in range(TURN):
            bca[r, 0] = jnp.broadcast_to(ca[0][:, r : r + 1], (8, 128))
            bca[r, 1] = jnp.broadcast_to(cab[0][:, r : r + 1], (8, 128))
        for t in range(TILES):
            scale2[t] = power_of(expo2[t])
            prev[t] = jnp.zeros((8, 128), F32)
            cur[t] = jnp.zeros((8, 128), F32)

        pos = lax.broadcasted_iota(jnp.int32, (16, DEG), 1)
        pos_even = (pos & 1) == 0
        narrow = lax.broadcasted_iota(jnp.int32, (16, 128), 1)

        def place(p, _):
            first = ord_ref[base + 2 * p]
            odd_first = first & 1
            e = jnp.where(odd_first == 0, first, DEG - 1 - first)
            pads = [jnp.zeros((4, DEG), F32)]
            da = jnp.concatenate([spec_ref[c, 0, 2 * p + odd_first].astype(F32) for c in range(COMPS)] + pads, axis=0)
            db = jnp.concatenate([spec_ref[c, 0, 2 * p + 1 - odd_first].astype(F32) for c in range(COMPS)] + pads, axis=0)
            da = da * jnp.where(e == 0, 1.0, 2.0)
            db = db * 2.0
            last = jnp.broadcast_to(db[:, DEG - 1 : DEG], (16, 128))
            lt[pl.ds(pl.multiple_of(16 * p, 16), 16), :] = jnp.where(narrow == p, last, 0.0).astype(BF16)
            da = pltpu.roll(da, jnp.where(e == 0, 0, DEG - e), 1)
            db = pltpu.roll(db, 1, 1)
            da = jnp.where(pos < DEG - e, da, 0.0)
            db = jnp.where(pos >= DEG - e, db, 0.0)
            lhs[p, 0:16] = jnp.where(pos_even, da, 0.0).astype(BF16)
            lhs[p, 16:32] = jnp.where(pos_even, 0.0, da).astype(BF16)
            lhs[p, 32:48] = jnp.where(pos_even, db, 0.0).astype(BF16)
            lhs[p, 48:64] = jnp.where(pos_even, 0.0, db).astype(BF16)
            return 0

        lax.fori_loop(0, PAIRS, place, 0)

    @pl.when(step == 1)
    def _():
        acc[...] = jnp.zeros_like(acc)

    new_half, old_half = lax.rem(step, 2), lax.rem(step + 1, 2)
    back = jnp.maximum(step - 1, 0)

    def advance(i, starts):
        rows = pl.ds(i * LSTRIDE, LB)
        left = lhs[i, :, pl.ds(pl.multiple_of(back * LB, LB), LB)]
        for half in range(2):
            table = jnp.concatenate([ft[old_half, 2 * half, rows, :], ft[old_half, 2 * half + 1, rows, :]], axis=1).astype(BF16)
            tab_ref[i, :, 256 * half : 256 * half + 256] = table
            acc[i, half] += jnp.dot(left, table, preferred_element_type=F32)

        xs = [jnp.broadcast_to(lat_ref[0:1, pl.ds(128 * t, 128)], (8, 128)) for t in range(TILES)]
        ps, cs, scales = [prev[t] for t in range(TILES)], [cur[t] for t in range(TILES)], [None] * TILES
        es = [expo[t] for t in range(TILES)]
        for k in range(2):
            use, make = (bca, bcb) if k == 0 else (bcb, bca)
            chunk = step * TURNS + 2 * i + k
            av, abv = ca[chunk + 1], cab[chunk + 1]
            for r in range(TURN):
                if r % 8 == 0:
                    for t in range(TILES):
                        big = jnp.abs(cs[t]) > BIG
                        f = jnp.where(big, SMALL, 1.0)
                        es[t] = jnp.where(big, es[t] + 40.0, es[t])
                        scales[t] = power_of(es[t])
                        ps[t], cs[t] = ps[t] * f, cs[t] * f
                make[r, 0] = jnp.broadcast_to(av[:, r : r + 1], (8, 128))
                make[r, 1] = jnp.broadcast_to(abv[:, r : r + 1], (8, 128))
                a, ab = use[r, 0], use[r, 1]
                if starts:
                    now = (chunk * TURN + r).astype(F32)
                    hit = mark[...] == now
                for t in range(TILES):
                    new = (a * xs[t]) * cs[t] - ab * ps[t]
                    if starts:
                        new = jnp.where(hit, ini2[t], new)
                        es[t] = jnp.where(hit, expo2[t], es[t])
                        scales[t] = jnp.where(hit, scale2[t], scales[t])
                        if r == 0 and k == 0:
                            new = jnp.where(jnp.full((8, 128), now) == 0.0, ini[t], new)
                    ps[t], cs[t] = cs[t], new
                    ft[new_half, t, pl.ds(2 * TURN * i + TURN * k + r, 8, stride=LSTRIDE), :] = new * scales[t]
        for t in range(TILES):
            prev[t], cur[t], expo[t] = ps[t], cs[t], es[t]

    def body(i, _):
        starting = flag[step * PAIRS + i] == 1

        @pl.when(starting)
        def _():
            advance(i, True)

        @pl.when(jnp.logical_not(starting))
        def _():
            advance(i, False)

        return 0

    lax.fori_loop(0, PAIRS, body, 0)

    @pl.when(step == STEPS - 1)
    def _():
        tail = jnp.concatenate([ft[new_half, t, pl.ds(0, 8, stride=LSTRIDE), :] for t in range(TILES)], axis=1)
        tailb[...] = jnp.concatenate([tail, jnp.zeros((8, HALF), F32)], axis=0).astype(BF16)
        tail_ref[...] = tailb[...]

        def spread(p, _):
            extra = jnp.dot(lt[pl.ds(pl.multiple_of(16 * p, 16), 16), 0:16], tailb[...], preferred_element_type=F32)
            for t in range(TILES):
                cols = slice(128 * (t % 2), 128 * (t % 2) + 128)
                part = acc[p, t // 2]
                for par in range(2):
                    sym, anti = part[32 * par : 32 * par + 16, cols], part[32 * par + 16 : 32 * par + 32, cols]
                    if par:
                        sym = sym + extra[:, 128 * t : 128 * t + 128]
                    ns[t, pl.ds(par * 8 + p, 16, stride=16), :] = sym + anti
                    ns[TILES + t, pl.ds(par * 8 + p, 16, stride=16), :] = sym - anti
            return 0

        lax.fori_loop(0, PAIRS, spread, 0)
        lane = lax.broadcasted_iota(jnp.int32, (8, 128), 1)
        for t in range(2 * TILES):
            near, far = ns[t, 0:128].T, ns[t, 128:256].T
            moved = pltpu.roll(far, 64, 1)
            for b in range(8):
                d = (t % TILES) * 8 + b
                dest = d if t < TILES else BLK - 1 - d
                msg_ref[dest, 0:16] = near[16 * b : 16 * b + 16].astype(BF16)
                msg_ref[dest, 16:24] = jnp.where(lane < 64, far[16 * b : 16 * b + 8], moved[16 * b + 8 : 16 * b + 16]).astype(BF16)


def run_legendre(order_map, lat, g, spec):
    full = lambda shape: pl.BlockSpec(shape, lambda i: (0,) * len(shape))
    return pl.pallas_call(
        legendre_kernel,
        grid=(STEPS,),
        in_specs=[
            pl.BlockSpec(memory_space=pltpu.SMEM),
            full((8, HALF)),
            full((1, DEG)),
            full((COMPS, 1, ORDERS, PARTS, DEG)),
        ],
        out_specs=[
            pl.BlockSpec((PAIRS, LB, HALF), lambda i: (0, jnp.maximum(i - 1, 0), 0)),
            full((16, HALF)),
            full((BLK, 24, 128)),
        ],
        out_shape=[
            jax.ShapeDtypeStruct((PAIRS, DEG, HALF), BF16),
            jax.ShapeDtypeStruct((16, HALF), BF16),
            jax.ShapeDtypeStruct((BLK, 24, 128), BF16),
        ],
        scratch_shapes=[
            pltpu.VMEM((STEPS * TURNS + 128 // TURN, 8, 128), F32),
            pltpu.VMEM((STEPS * TURNS + 128 // TURN, 8, 128), F32),
            pltpu.VMEM((TILES, 8, 128), F32),
            pltpu.VMEM((TILES, 8, 128), F32),
            pltpu.VMEM((TILES, 8, 128), F32),
            pltpu.VMEM((TILES, 8, 128), F32),
            pltpu.VMEM((TILES, 8, 128), F32),
            pltpu.VMEM((TILES, 8, 128), F32),
            pltpu.VMEM((TILES, 8, 128), F32),
            pltpu.VMEM((8, 128), F32),
            pltpu.VMEM((TURN, 2, 8, 128), F32),
            pltpu.VMEM((TURN, 2, 8, 128), F32),
            pltpu.VMEM((2, TILES, PAIRS * LSTRIDE + 8, 128), F32),
            pltpu.VMEM((PAIRS, 2, 64, 256), F32),
            pltpu.VMEM((PAIRS, 64, DEG), BF16),
            pltpu.VMEM((128, 128), BF16),
            pltpu.VMEM((16, HALF), BF16),
            pltpu.VMEM((2 * TILES, 256, 128), F32),
            pltpu.SMEM((STEPS * PAIRS,), jnp.int32),
        ],
        name="legendre",
    )(order_map, lat, g, spec)


def turn(phase):
    t = phase * (1.0 / KH) - 1.0
    z = t * t
    c = jnp.full_like(z, 0.0)
    s = jnp.full_like(z, 0.0)
    for i in range(8, -1, -1):
        c = c * z + float((-1) ** (i + 1) * math.pi ** (2 * i) / math.factorial(2 * i))
        s = s * z + float((-1) ** (i + 1) * math.pi ** (2 * i + 1) / math.factorial(2 * i + 1))
    return c, s * t


def wrap(value):
    return value - POINTS * jnp.floor(value * (1.0 / POINTS))


def turned(value, quarters):
    return pltpu.roll(value, (32 * quarters) % 128, 1) if quarters % 4 else value


def tail_kernel(
    ord_ref, rad_ref, shift_ref, vis_ref, lat_ref, last_ref, msg_ref, tab_hbm, out_ref, sum_ref,
    tab, wave, left, pm, vis, got, give, back, side, part, held, near, pass_on, far, sems, pair_sems,
):
    here = lax.axis_index("blk")
    shell = lax.axis_index("shell")
    layer, core = shell // 2, lax.rem(shell, 2)
    partner, across = 2 * layer + 1 - core, 2 * (1 - layer) + core
    load = pltpu.make_async_copy(tab_hbm, tab, sems.at[5])
    load.start()
    barrier = pltpu.get_barrier_semaphore()

    def greet(i, _):
        pl.semaphore_signal(barrier, inc=1, device_id={"blk": lax.rem(here + i, BLK)}, device_id_type=MESH)
        return 0

    lax.fori_loop(1, BLK, greet, 0)
    for peer in (partner, across):
        pl.semaphore_signal(barrier, inc=1, device_id={"shell": peer}, device_id_type=MESH)

    lane = lax.broadcasted_iota(jnp.int32, (8, 128), 1).astype(F32)
    sub8 = lax.broadcasted_iota(jnp.int32, (8, 128), 0)
    sc, ss = [], []
    for u in range(KH // 128):
        sc.append(jnp.broadcast_to(shift_ref[0:1, pl.ds(128 * u, 128)], (8, 128)))
        ss.append(jnp.broadcast_to(shift_ref[1:2, pl.ds(128 * u, 128)], (8, 128)))

    def make(src, _):
        even = jnp.zeros((8, 128), jnp.int32)
        for p in range(PAIRS):
            first = ord_ref[src * ORDERS + 2 * p]
            even = jnp.where(sub8 == p, jnp.where((first & 1) == 0, first, DEG - 1 - first), even)
        m = even.astype(F32)
        c, s = turn(wrap(m * lane))
        gc, gs = turn(wrap(m * 128.0))
        for u in range(KH // 128):
            oc = sc[u] * c - ss[u] * s
            os = -(ss[u] * c + sc[u] * s)
            rows = pl.ds(pl.multiple_of(src * 32, 32), 32)
            wave[rows, pl.ds(128 * u, 128)] = jnp.concatenate([c, oc, -s, -os], axis=0).astype(BF16)
            c, s = c * gc - s * gs, s * gc + c * gs
        return 0

    lax.fori_loop(0, EARLY, make, 0)
    pl.semaphore_wait(barrier, BLK + 1)

    def send_first(i, _):
        peer = lax.rem(here + i, BLK)
        pltpu.make_async_remote_copy(
            src_ref=msg_ref.at[peer], dst_ref=got.at[here], send_sem=sems.at[0], recv_sem=sems.at[1],
            device_id={"blk": peer}, device_id_type=MESH,
        ).start()
        return 0

    lax.fori_loop(1, BLK, send_first, 0)
    own = pltpu.make_async_copy(msg_ref.at[here], got.at[here], sems.at[4])
    own.start()
    lax.fori_loop(EARLY, BLK, make, 0)

    for j in range(CYC):
        row = jnp.where(here >= BLK // 2, CYC - 1 - j, j)
        vis[j : j + 1, :] = vis_ref[0, pl.ds(row, 1), :]

    own.wait()
    pltpu.make_async_remote_copy(
        src_ref=msg_ref.at[0 : BLK - 1], dst_ref=got.at[0 : BLK - 1], send_sem=sems.at[0], recv_sem=sems.at[1],
        device_id={"blk": here}, device_id_type=MESH,
    ).wait()

    wide = lax.broadcasted_iota(jnp.int32, (16, 128), 1)
    even = ((wide // 8) % 2) == 0
    quarter = wide // 32
    for g in range(BLK // 4):
        pieces = [(got[4 * g + i, 0:16].astype(F32), got[4 * g + i, 16:24].astype(F32)) for i in range(4)]
        for c in range(COMPS):
            total = None
            for i in range(4):
                first, rest = pieces[i]
                moved = turned(first, i - c) if c < 4 else jnp.concatenate([turned(rest, i - c), turned(rest, i - c - 2)], axis=0)
                total = moved if total is None else jnp.where(quarter == i, moved, total)
            left[16 * c : 16 * c + 16, pl.ds(128 * g, 128)] = jnp.where(even, total, 0.0).astype(BF16)
            left[96 + 16 * c : 112 + 16 * c, pl.ds(128 * g, 128)] = jnp.where(even, 0.0, total).astype(BF16)

    for u in range(KH // 256):
        cols = pl.ds(256 * u, 256)
        field = jnp.dot(left[...], wave[:, cols], preferred_element_type=F32)
        low, high = vis[:, cols], vis[:, pl.ds(KH + 256 * u, 256)]
        for c in range(COMPS):
            e, o = field[16 * c : 16 * c + 16], field[96 + 16 * c : 112 + 16 * c]
            first, second = low * (e + o), high * (e - o)
            pm[16 * c : 16 * c + 16, cols] = (first + second).astype(BF16)
            pm[96 + 16 * c : 112 + 16 * c, cols] = (first - second).astype(BF16)

    lanes = lax.broadcasted_iota(jnp.int32, (96, 256), 1)
    pick = ((lanes // 8) % 2) == 0

    def send_block(blk):
        for i in range(8):
            peer = blk * 8 + i

            @pl.when(peer != here)
            def _():
                pltpu.make_async_remote_copy(
                    src_ref=give.at[peer], dst_ref=back.at[here], send_sem=sems.at[2], recv_sem=sems.at[3],
                    device_id={"blk": peer}, device_id_type=MESH,
                ).start()

    def block_of(b):
        return lax.rem(b + here // 8, 8)

    def spectra(b, _):
        blk = block_of(b)
        rows = pl.ds(pl.multiple_of(blk * 256, 256), 256)
        both = lax.dot_general(pm[...], wave[rows, :], NT, preferred_element_type=F32)
        spect = jnp.where(pick, both[:96], both[96:]) * (2.0 * math.pi / POINTS)
        for g in range(2):
            vals = [spect[16 * c : 16 * c + 16, 128 * g : 128 * g + 128] for c in range(COMPS)]
            for i in range(4):
                low = None
                for c in range(4):
                    moved = turned(vals[c], c - i)
                    low = moved if low is None else jnp.where(quarter == c, moved, low)
                high = None
                for c in range(4):
                    moved = turned(vals[4 + c % 2][8 * (c // 2) : 8 * (c // 2) + 8], c - i)
                    high = moved if high is None else jnp.where(quarter[:8] == c, moved, high)
                give[blk * 8 + 4 * g + i, 0:16] = low.astype(BF16)
                give[blk * 8 + 4 * g + i, 16:24] = high.astype(BF16)

        @pl.when(b > 0)
        def _():
            send_block(block_of(b + 7))

        return 0

    lax.fori_loop(0, 8, spectra, 0)
    send_block(block_of(7))
    own = pltpu.make_async_copy(give.at[here], back.at[here], sems.at[4])
    own.start()
    own.wait()
    load.wait()
    pltpu.make_async_remote_copy(
        src_ref=give.at[0 : BLK - 1], dst_ref=back.at[0 : BLK - 1], send_sem=sems.at[2], recv_sem=sems.at[3],
        device_id={"blk": here}, device_id_type=MESH,
    ).wait()

    def fetch(d):
        first, rest = back[d, 0:16].astype(F32), back[d, 16:24].astype(F32)
        return first, jnp.concatenate([rest, pltpu.roll(rest, 64, 1)], axis=0)

    for t in range(TILES):
        w = lat_ref[3:4, pl.ds(128 * t, 128)]
        north = [fetch(8 * t + b) for b in range(8)]
        south = [fetch(BLK - 1 - 8 * t - b) for b in range(8)]
        for h in range(2):
            up = jnp.concatenate([v[h] for v in north], axis=0)
            down = jnp.concatenate([v[h] for v in south], axis=0)
            side[t, 0, pl.ds(128 * h, 128), :] = (up + down).T * w
            side[t, 1, pl.ds(128 * h, 128), :] = (up - down).T * w

    share = DEG // SHELLS
    pos = lax.broadcasted_iota(jnp.int32, (16, DEG), 1)
    pos_even = (pos & 1) == 0
    tiny = lax.broadcasted_iota(jnp.int32, (16, 16), 1)

    def near_copy(k, p):
        return pltpu.make_async_remote_copy(
            src_ref=part.at[k, p], dst_ref=near.at[k, p], send_sem=pair_sems.at[0, k, p], recv_sem=pair_sems.at[1, k, p],
            device_id={"shell": partner}, device_id_type=MESH,
        )

    def far_copy(p):
        return pltpu.make_async_remote_copy(
            src_ref=pass_on.at[p], dst_ref=far.at[p], send_sem=pair_sems.at[2, 0, p], recv_sem=pair_sems.at[2, 1, p],
            device_id={"shell": across}, device_id_type=MESH,
        )

    def forward(p):
        near_copy(0, p).wait_recv()
        pass_on[p] = (held[0, p] + near[0, p].astype(F32)).astype(BF16)
        far_copy(p).start()

    def analyse(p, _):
        first = ord_ref[here * ORDERS + 2 * p]
        odd_first = first & 1
        e = jnp.where(odd_first == 0, first, DEG - 1 - first)
        rows = jnp.concatenate(
            [
                jnp.concatenate([side[t, half, pl.ds(8 * par + p, 16, stride=16), :] for t in range(TILES)], axis=1)
                for par in range(2)
                for half in range(2)
            ],
            axis=0,
        ).astype(BF16)
        both = lax.dot_general(rows, tab[p], NT, preferred_element_type=F32)
        final = lax.dot_general(rows[32:48], last_ref[...], NT, preferred_element_type=F32)
        final = jnp.sum(jnp.where(tiny == p, final, 0.0), axis=1, keepdims=True)
        ca = jnp.where(pos_even, both[0:16], both[16:32])
        cb = jnp.where(pos_even, both[32:48], both[48:64])
        ca = jnp.where(pos >= e, pltpu.roll(ca, e, 1), 0.0)
        cb = jnp.where(pos >= DEG - 1 - e, pltpu.roll(cb, DEG - 1, 1), 0.0)
        cb = jnp.where(pos == DEG - 1, final, cb)
        keep = jnp.full((16, DEG), odd_first) == 0
        pair = (jnp.where(keep, ca, cb), jnp.where(keep, cb, ca))
        for k in range(2):
            for c in range(COMPS):
                out_ref[c, 0, 2 * p + k] = pair[k][2 * c : 2 * c + 2].astype(BF16)
        scaled = jnp.concatenate([pair[0][0:12], pair[1][0:12]], axis=0) * rad_ref[0]
        for layer_index in range(2):
            for core_index in range(2):
                piece = scaled[:, share * (2 * layer_index + core_index) : share * (2 * layer_index + core_index + 1)]
                is_across = layer_index != layer
                k = jnp.where(is_across, 0, 1)

                @pl.when(core_index == core)
                def _():
                    held[k, p] = piece

                @pl.when(core_index != core)
                def _():
                    part[k, p] = piece.astype(BF16)

        near_copy(0, p).start()
        near_copy(1, p).start()

        @pl.when(p > 0)
        def _():
            forward(p - 1)

        return 0

    lax.fori_loop(0, PAIRS, analyse, 0)
    forward(PAIRS - 1)

    def finish(p, _):
        near_copy(1, p).wait_recv()
        total = held[1, p] + near[1, p].astype(F32)
        far_copy(p).wait_recv()
        total = total + far[p].astype(F32)
        for k in range(2):
            for c in range(COMPS):
                sum_ref[c, 2 * p + k] = total[12 * k + 2 * c : 12 * k + 2 * c + 2]
        near_copy(0, p).wait_send()
        near_copy(1, p).wait_send()
        far_copy(p).wait_send()
        return 0

    lax.fori_loop(0, PAIRS, finish, 0)


def run_tail(order_map, rad, shift, vis, lat, last, msg, tab):
    smem, vmem = pl.BlockSpec(memory_space=pltpu.SMEM), pl.BlockSpec(memory_space=pltpu.VMEM)
    share = DEG // SHELLS
    block = (PAIRS, 24, share)
    return pl.pallas_call(
        tail_kernel,
        in_specs=[smem, smem, vmem, vmem, vmem, vmem, vmem, pl.BlockSpec(memory_space=pl.ANY)],
        out_specs=[vmem, vmem],
        out_shape=[
            jax.ShapeDtypeStruct((COMPS, 1, ORDERS, PARTS, DEG), BF16),
            jax.ShapeDtypeStruct((COMPS, ORDERS, PARTS, share), F32),
        ],
        scratch_shapes=[
            pltpu.VMEM((PAIRS, DEG, HALF), BF16),
            pltpu.VMEM((POINTS, KH), BF16),
            pltpu.VMEM((192, POINTS), BF16),
            pltpu.VMEM((192, KH), BF16),
            pltpu.VMEM((CYC, POINTS), F32),
            pltpu.VMEM((BLK, 24, 128), BF16),
            pltpu.VMEM((BLK, 24, 128), BF16),
            pltpu.VMEM((BLK, 24, 128), BF16),
            pltpu.VMEM((TILES, 2, 256, 128), F32),
            pltpu.VMEM((2,) + block, BF16),
            pltpu.VMEM((2,) + block, F32),
            pltpu.VMEM((2,) + block, BF16),
            pltpu.VMEM(block, BF16),
            pltpu.VMEM(block, BF16),
            pltpu.SemaphoreType.DMA((6,)),
            pltpu.SemaphoreType.DMA((3, 2, PAIRS)),
        ],
        compiler_params=pltpu.CompilerParams(collective_id=0, has_side_effects=True),
        name="tail",
    )(order_map, rad, shift, vis, lat, last, msg, tab)


def shift_table():
    k = np.arange(KH, dtype=np.float64)
    ang = 2.0 * np.pi * k / POINTS
    sign = 1.0 - 2.0 * (k % 2)
    return np.stack([sign * np.cos(ang), sign * np.sin(ang)]).astype(np.float32)


def shards(strain_spec, order_map, viscosity, radial_weight):
    lat, g = latitude_constants()
    lat, g = jnp.asarray(lat), jnp.asarray(g)
    tab, last, msg = run_legendre(order_map, lat, g, strain_spec)
    return run_tail(order_map, radial_weight, jnp.asarray(shift_table()), viscosity, lat, last, msg, tab)


def solution(mesh):
    return jax.shard_map(
        shards,
        mesh=mesh,
        in_specs=(P(None, "shell", "blk", None, None), P(), P("shell", "blk", None), P("shell")),
        out_specs=(P(None, "shell", "blk", None, None), P(None, "blk", None, "shell")),
        check_vma=False,
    )
```

```python
import math

import jax
import jax.numpy as jnp
import numpy as np
from jax import lax
from jax.experimental import pallas as pl
from jax.experimental.pallas import tpu as pltpu
from jax.sharding import PartitionSpec as P

F32 = jnp.float32
BF16 = jnp.bfloat16
COMPS = 6
PARTS = 2
ORDERS = 16
DEG = 1024
HALF = 512
BLK = 64
SHELLS = 4
CYC = 16
POINTS = 2048
KH = POINTS // 2
LB = 256
LSTRIDE = LB + 1
TILES = HALF // 128
PAIRS = 8
TURN = 16
TURNS = LB // TURN
WIDE = DEG + 128
BIG = 2.0**40
SMALL = 2.0**-40
NT = (((1,), (1,)), ((), ()))
MESH = pl.DeviceIdType.MESH


def latitude_constants():
    j = np.arange(HALF, dtype=np.float64)
    theta = np.pi * (2.0 * j + 1.0) / (4.0 * HALF)
    x = np.cos(theta)
    logsin = np.log2(np.sin(theta))
    hi = np.round(logsin * 512.0) / 512.0
    lo = logsin - hi
    k = np.arange(1, HALF + 1, dtype=np.float64)
    phase = np.outer(k, 2.0 * j + 1.0) % (4.0 * HALF)
    series = np.sum(np.cos(phase * np.pi / (2.0 * HALF)) / (4.0 * k * k - 1.0)[:, None], axis=0)
    weight = (2.0 / (2.0 * HALF)) * (1.0 - 2.0 * series)
    m = np.arange(DEG, dtype=np.float64)
    fac = np.concatenate([[0.0], np.cumsum(np.log2(1.0 - 0.5 / np.arange(1, DEG)))])
    g = 0.5 * np.log2((2.0 * m + 1.0) / (4.0 * np.pi)) + 0.5 * fac
    lat = np.stack([x, hi, lo, weight]).astype(np.float32)
    return np.concatenate([lat, np.zeros((4, HALF), np.float32)]), g.astype(np.float32)[None]


def power_of(e):
    return jnp.where(e < -126.0, 0.0, jnp.exp(jnp.maximum(e, -126.0) * math.log(2.0)))


def legendre_init(ord_ref, lat_ref, g_ref, base, ca, cab, ini, expo, ini2, expo2, mark, bca):
    sub8 = lax.broadcasted_iota(jnp.int32, (8, 128), 0)
    even = jnp.zeros((8, 128), jnp.int32)
    for p in range(PAIRS):
        first = ord_ref[base + 2 * p]
        even = jnp.where(sub8 == p, jnp.where((first & 1) == 0, first, DEG - 1 - first), even)
    ma = even.astype(F32)
    mb = (DEG - 1.0) - ma
    delta = (even & 7).astype(F32) + 1.0
    start = mb + delta
    mark[...] = start
    lane = lax.broadcasted_iota(jnp.int32, (8, 128), 1).astype(F32)
    for b in range(DEG // 128 + 1):
        t = lane + float(128 * b)
        second = t >= start
        m = jnp.where(second, mb, ma)
        l = jnp.where(second, t - delta, t + ma)
        up = (l > m) & (l < DEG - 0.5)
        a2 = (4.0 * l * l - 1.0) / jnp.where(up, (l - m) * (l + m), 1.0)
        a = jnp.where(up, jnp.sqrt(jnp.where(up, a2, 1.0)), 0.0)
        below = l - 1.0
        top = jnp.where(below > m, (below - m) * (below + m), 0.0)
        ab = a * jnp.sqrt(top / jnp.maximum(4.0 * below * below - 1.0, 1.0))
        for k in range(128 // TURN):
            ca[b * (128 // TURN) + k] = pltpu.roll(a, (128 - TURN * k) % 128, 1)
            cab[b * (128 // TURN) + k] = pltpu.roll(ab, (128 - TURN * k) % 128, 1)
    glane = lax.broadcasted_iota(jnp.int32, (8, DEG), 1).astype(F32)
    for m, first, power in ((ma, ini, expo), (mb, ini2, expo2)):
        gm = jnp.sum(jnp.where(glane == m[:, :1], g_ref[...], 0.0), axis=1, keepdims=True)
        for t in range(TILES):
            cols = pl.ds(128 * t, 128)
            mh = m * lat_ref[1:2, cols]
            whole = jnp.floor(mh)
            first[t] = jnp.exp(((mh - whole) + m * lat_ref[2:3, cols] + gm) * math.log(2.0))
            power[t] = whole
    for r in range(TURN):
        bca[r, 0] = jnp.broadcast_to(ca[0][:, r : r + 1], (8, 128))
        bca[r, 1] = jnp.broadcast_to(cab[0][:, r : r + 1], (8, 128))


def place_pairs(ord_ref, spec_ref, base, lhs):
    pos = lax.broadcasted_iota(jnp.int32, (16, WIDE), 1)
    pos_even = (pos & 1) == 0

    def place(p, _):
        first = ord_ref[base + 2 * p]
        odd_first = first & 1
        e = jnp.where(odd_first == 0, first, DEG - 1 - first)
        pads = [jnp.zeros((4, DEG), F32)]
        empty = jnp.zeros((16, WIDE - DEG), F32)
        da = jnp.concatenate([spec_ref[c, 0, 2 * p + odd_first].astype(F32) for c in range(COMPS)] + pads, axis=0)
        db = jnp.concatenate([spec_ref[c, 0, 2 * p + 1 - odd_first].astype(F32) for c in range(COMPS)] + pads, axis=0)
        da = da * jnp.where(e == 0, 1.0, 2.0)
        db = jnp.concatenate([db * 2.0, empty], axis=1)
        da = jnp.concatenate([pltpu.roll(da, jnp.where(e == 0, 0, DEG - e), 1), empty], axis=1)
        db = pltpu.roll(db, (e & 7) + 1, 1)
        da = jnp.where(pos < DEG - e, da, 0.0)
        db = jnp.where(pos >= DEG - e + (e & 7), db, 0.0)
        lhs[p, 0:16] = jnp.where(pos_even, da, 0.0).astype(BF16)
        lhs[p, 16:32] = jnp.where(pos_even, 0.0, da).astype(BF16)
        lhs[p, 32:48] = jnp.where(pos_even, db, 0.0).astype(BF16)
        lhs[p, 48:64] = jnp.where(pos_even, 0.0, db).astype(BF16)
        return 0

    lax.fori_loop(0, PAIRS, place, 0)


def legendre_synthesis(ord_ref, lat_ref, g_ref, spec_ref, base, tab, tail, msg, refs):
    ca, cab, prev, cur, expo, ini, ini2, expo2, mark, bca, bcb, ft, acc, lhs, ns = refs
    legendre_init(ord_ref, lat_ref, g_ref, base, ca, cab, ini, expo, ini2, expo2, mark, bca)
    place_pairs(ord_ref, spec_ref, base, lhs)
    for t in range(TILES):
        prev[t] = jnp.zeros((8, 128), F32)
        cur[t] = jnp.zeros((8, 128), F32)
    acc[...] = jnp.zeros_like(acc)

    def multiply(block, i):
        rows = pl.ds(i * LSTRIDE, LB)
        half_index = lax.rem(block, 2)
        span = pl.ds(pl.multiple_of(block * LB, LB), LB)
        left = lhs[i, :, span]
        for half in range(2):
            table = jnp.concatenate([ft[half_index, 2 * half, rows, :], ft[half_index, 2 * half + 1, rows, :]], axis=1)
            table = table.astype(BF16)
            tab[i, span, 256 * half : 256 * half + 256] = table
            acc[i, half] += jnp.dot(left, table, preferred_element_type=F32)

    def recur(block, i, turns, opening):
        half_index = lax.rem(block, 2)
        xs = [jnp.broadcast_to(lat_ref[0:1, pl.ds(128 * t, 128)], (8, 128)) for t in range(TILES)]
        ps, cs, scales = [prev[t] for t in range(TILES)], [cur[t] for t in range(TILES)], [None] * TILES
        es = [expo[t] for t in range(TILES)]
        for k in range(turns):
            use, make = (bca, bcb) if k == 0 else (bcb, bca)
            chunk = block * TURNS + 2 * i + k
            av, abv = ca[chunk + 1], cab[chunk + 1]
            for r in range(TURN):
                if r % 8 == 0:
                    now = jnp.full((8, 128), chunk * TURN + r).astype(F32)
                    hit = mark[...] == now
                    for t in range(TILES):
                        big = jnp.abs(cs[t]) > BIG
                        f = jnp.where(big, SMALL, 1.0)
                        es[t] = jnp.where(hit, expo2[t], jnp.where(big, es[t] + 40.0, es[t]))
                        scales[t] = power_of(es[t])
                        ps[t], cs[t] = ps[t] * f, cs[t] * f
                if turns == 2:
                    make[r, 0] = jnp.broadcast_to(av[:, r : r + 1], (8, 128))
                    make[r, 1] = jnp.broadcast_to(abv[:, r : r + 1], (8, 128))
                a, ab = use[r, 0], use[r, 1]
                for t in range(TILES):
                    new = (a * xs[t]) * cs[t] - ab * ps[t]
                    if r % 8 == 0:
                        new = jnp.where(hit, ini2[t], new)
                        if opening and r == 0 and k == 0:
                            new = jnp.where(now == 0.0, ini[t], new)
                    ps[t], cs[t] = cs[t], new
                    ft[half_index, t, pl.ds(2 * TURN * i + TURN * k + r, 8, stride=LSTRIDE), :] = new * scales[t]
        for t in range(TILES):
            prev[t], cur[t], expo[t] = ps[t], cs[t], es[t]

    def first_block(i, _):
        recur(0, i, 2, True)
        return 0

    def middle(n, _):
        block, i = n // PAIRS, lax.rem(n, PAIRS)
        multiply(block - 1, i)
        recur(block, i, 2, False)
        return 0

    lax.fori_loop(0, PAIRS, first_block, 0)
    lax.fori_loop(PAIRS, PAIRS * (DEG // LB), middle, 0)
    recur(DEG // LB, 0, 1, False)

    def last_block(i, _):
        multiply(DEG // LB - 1, i)
        rows = pl.ds(i * LSTRIDE, 16)
        table = jnp.concatenate([ft[0, t, rows, :] for t in range(TILES)], axis=1).astype(BF16)
        tail[i] = table
        extra = jnp.dot(lhs[i, 32:64, DEG:WIDE][:, 0:16], table, preferred_element_type=F32)
        for t in range(TILES):
            cols = slice(128 * (t % 2), 128 * (t % 2) + 128)
            part = acc[i, t // 2]
            for par in range(2):
                sym, anti = part[32 * par : 32 * par + 16, cols], part[32 * par + 16 : 32 * par + 32, cols]
                if par:
                    sym = sym + extra[0:16, 128 * t : 128 * t + 128]
                    anti = anti + extra[16:32, 128 * t : 128 * t + 128]
                ns[t, pl.ds(par * 8 + i, 16, stride=16), :] = sym + anti
                ns[TILES + t, pl.ds(par * 8 + i, 16, stride=16), :] = sym - anti
        return 0

    lax.fori_loop(0, PAIRS, last_block, 0)
    lane = lax.broadcasted_iota(jnp.int32, (8, 128), 1)
    for t in range(2 * TILES):
        near, far = ns[t, 0:128].T, ns[t, 128:256].T
        moved = pltpu.roll(far, 64, 1)
        for b in range(8):
            d = (t % TILES) * 8 + b
            dest = d if t < TILES else BLK - 1 - d
            msg[dest, 0:16] = near[16 * b : 16 * b + 16].astype(BF16)
            msg[dest, 16:24] = jnp.where(lane < 64, far[16 * b : 16 * b + 8], moved[16 * b + 8 : 16 * b + 16]).astype(BF16)


def turn(phase):
    t = phase * (1.0 / KH) - 1.0
    z = t * t
    c = jnp.full_like(z, 0.0)
    s = jnp.full_like(z, 0.0)
    for i in range(8, -1, -1):
        c = c * z + float((-1) ** (i + 1) * math.pi ** (2 * i) / math.factorial(2 * i))
        s = s * z + float((-1) ** (i + 1) * math.pi ** (2 * i + 1) / math.factorial(2 * i + 1))
    return c, s * t


def wrap(value):
    return value - POINTS * jnp.floor(value * (1.0 / POINTS))


def turned(value, quarters):
    return pltpu.roll(value, (32 * quarters) % 128, 1) if quarters % 4 else value


def whole_kernel(
    ord_ref, rad_ref, shift_ref, vis_ref, lat_ref, g_ref, spec_ref, out_ref, sum_ref,
    tab, last_ref, msg_ref, wave, left, pm, vis, got, give, back, side, part, held, near, pass_on, far, sems, pair_sems, *refs,
):
    here = lax.axis_index("blk")
    shell = lax.axis_index("shell")
    layer, core = shell // 2, lax.rem(shell, 2)
    partner, across = 2 * layer + 1 - core, 2 * (1 - layer) + core
    barrier = pltpu.get_barrier_semaphore()

    def greet(i, _):
        pl.semaphore_signal(barrier, inc=1, device_id={"blk": lax.rem(here + i, BLK)}, device_id_type=MESH)
        return 0

    lax.fori_loop(1, BLK, greet, 0)
    for peer in (partner, across):
        pl.semaphore_signal(barrier, inc=1, device_id={"shell": peer}, device_id_type=MESH)

    legendre_synthesis(ord_ref, lat_ref, g_ref, spec_ref, here * ORDERS, tab, last_ref, msg_ref, refs)
    pl.semaphore_wait(barrier, BLK + 1)

    def send_first(i, _):
        peer = lax.rem(here + i, BLK)
        pltpu.make_async_remote_copy(
            src_ref=msg_ref.at[peer], dst_ref=got.at[here], send_sem=sems.at[0], recv_sem=sems.at[1],
            device_id={"blk": peer}, device_id_type=MESH,
        ).start()
        return 0

    lax.fori_loop(1, BLK, send_first, 0)
    own = pltpu.make_async_copy(msg_ref.at[here], got.at[here], sems.at[4])
    own.start()

    lane = lax.broadcasted_iota(jnp.int32, (8, 128), 1).astype(F32)
    sub8 = lax.broadcasted_iota(jnp.int32, (8, 128), 0)
    sc, ss = [], []
    for u in range(KH // 128):
        sc.append(jnp.broadcast_to(shift_ref[0:1, pl.ds(128 * u, 128)], (8, 128)))
        ss.append(jnp.broadcast_to(shift_ref[1:2, pl.ds(128 * u, 128)], (8, 128)))

    def make(src, _):
        even = jnp.zeros((8, 128), jnp.int32)
        for p in range(PAIRS):
            first = ord_ref[src * ORDERS + 2 * p]
            even = jnp.where(sub8 == p, jnp.where((first & 1) == 0, first, DEG - 1 - first), even)
        m = even.astype(F32)
        c, s = turn(wrap(m * lane))
        gc, gs = turn(wrap(m * 128.0))
        for u in range(KH // 128):
            oc = sc[u] * c - ss[u] * s
            os = -(ss[u] * c + sc[u] * s)
            rows = pl.ds(pl.multiple_of(src * 32, 32), 32)
            wave[rows, pl.ds(128 * u, 128)] = jnp.concatenate([c, oc, -s, -os], axis=0).astype(BF16)
            c, s = c * gc - s * gs, s * gc + c * gs
        return 0

    lax.fori_loop(0, BLK, make, 0)
    for j in range(CYC):
        row = jnp.where(here >= BLK // 2, CYC - 1 - j, j)
        vis[j : j + 1, :] = vis_ref[0, pl.ds(row, 1), :]

    own.wait()
    pltpu.make_async_remote_copy(
        src_ref=msg_ref.at[0 : BLK - 1], dst_ref=got.at[0 : BLK - 1], send_sem=sems.at[0], recv_sem=sems.at[1],
        device_id={"blk": here}, device_id_type=MESH,
    ).wait()

    wide = lax.broadcasted_iota(jnp.int32, (16, 128), 1)
    even = ((wide // 8) % 2) == 0
    quarter = wide // 32
    for g in range(BLK // 4):
        pieces = [(got[4 * g + i, 0:16].astype(F32), got[4 * g + i, 16:24].astype(F32)) for i in range(4)]
        for c in range(COMPS):
            total = None
            for i in range(4):
                first, rest = pieces[i]
                moved = turned(first, i - c) if c < 4 else jnp.concatenate([turned(rest, i - c), turned(rest, i - c - 2)], axis=0)
                total = moved if total is None else jnp.where(quarter == i, moved, total)
            left[16 * c : 16 * c + 16, pl.ds(128 * g, 128)] = jnp.where(even, total, 0.0).astype(BF16)
            left[96 + 16 * c : 112 + 16 * c, pl.ds(128 * g, 128)] = jnp.where(even, 0.0, total).astype(BF16)

    for u in range(KH // 256):
        cols = pl.ds(256 * u, 256)
        field = jnp.dot(left[...], wave[:, cols], preferred_element_type=F32)
        low, high = vis[:, cols], vis[:, pl.ds(KH + 256 * u, 256)]
        for c in range(COMPS):
            e, o = field[16 * c : 16 * c + 16], field[96 + 16 * c : 112 + 16 * c]
            first, second = low * (e + o), high * (e - o)
            pm[16 * c : 16 * c + 16, cols] = (first + second).astype(BF16)
            pm[96 + 16 * c : 112 + 16 * c, cols] = (first - second).astype(BF16)

    lanes = lax.broadcasted_iota(jnp.int32, (96, 256), 1)
    pick = ((lanes // 8) % 2) == 0

    def send_block(blk):
        for i in range(8):
            peer = blk * 8 + i

            @pl.when(peer != here)
            def _():
                pltpu.make_async_remote_copy(
                    src_ref=give.at[peer], dst_ref=back.at[here], send_sem=sems.at[2], recv_sem=sems.at[3],
                    device_id={"blk": peer}, device_id_type=MESH,
                ).start()

    def block_of(b):
        return lax.rem(b + here // 8, 8)

    def spectra(b, _):
        blk = block_of(b)
        rows = pl.ds(pl.multiple_of(blk * 256, 256), 256)
        both = lax.dot_general(pm[...], wave[rows, :], NT, preferred_element_type=F32)
        spect = jnp.where(pick, both[:96], both[96:]) * (2.0 * math.pi / POINTS)
        for g in range(2):
            vals = [spect[16 * c : 16 * c + 16, 128 * g : 128 * g + 128] for c in range(COMPS)]
            for i in range(4):
                low = None
                for c in range(4):
                    moved = turned(vals[c], c - i)
                    low = moved if low is None else jnp.where(quarter == c, moved, low)
                high = None
                for c in range(4):
                    moved = turned(vals[4 + c % 2][8 * (c // 2) : 8 * (c // 2) + 8], c - i)
                    high = moved if high is None else jnp.where(quarter[:8] == c, moved, high)
                give[blk * 8 + 4 * g + i, 0:16] = low.astype(BF16)
                give[blk * 8 + 4 * g + i, 16:24] = high.astype(BF16)

        @pl.when(b > 0)
        def _():
            send_block(block_of(b + 7))

        return 0

    lax.fori_loop(0, 8, spectra, 0)
    send_block(block_of(7))
    own = pltpu.make_async_copy(give.at[here], back.at[here], sems.at[4])
    own.start()
    own.wait()
    pltpu.make_async_remote_copy(
        src_ref=give.at[0 : BLK - 1], dst_ref=back.at[0 : BLK - 1], send_sem=sems.at[2], recv_sem=sems.at[3],
        device_id={"blk": here}, device_id_type=MESH,
    ).wait()

    def fetch(d):
        first, rest = back[d, 0:16].astype(F32), back[d, 16:24].astype(F32)
        return first, jnp.concatenate([rest, pltpu.roll(rest, 64, 1)], axis=0)

    for t in range(TILES):
        w = lat_ref[3:4, pl.ds(128 * t, 128)]
        north = [fetch(8 * t + b) for b in range(8)]
        south = [fetch(BLK - 1 - 8 * t - b) for b in range(8)]
        for h in range(2):
            up = jnp.concatenate([v[h] for v in north], axis=0)
            down = jnp.concatenate([v[h] for v in south], axis=0)
            side[t, 0, pl.ds(128 * h, 128), :] = (up + down).T * w
            side[t, 1, pl.ds(128 * h, 128), :] = (up - down).T * w

    share = DEG // SHELLS
    pos = lax.broadcasted_iota(jnp.int32, (16, DEG), 1)
    pos_even = (pos & 1) == 0
    tiny_even = (lax.broadcasted_iota(jnp.int32, (16, 16), 1) & 1) == 0

    def near_copy(k, p):
        return pltpu.make_async_remote_copy(
            src_ref=part.at[k, p], dst_ref=near.at[k, p], send_sem=pair_sems.at[0, k, p], recv_sem=pair_sems.at[1, k, p],
            device_id={"shell": partner}, device_id_type=MESH,
        )

    def far_copy(p):
        return pltpu.make_async_remote_copy(
            src_ref=pass_on.at[p], dst_ref=far.at[p], send_sem=pair_sems.at[2, 0, p], recv_sem=pair_sems.at[2, 1, p],
            device_id={"shell": across}, device_id_type=MESH,
        )

    def forward(p):
        near_copy(0, p).wait_recv()
        pass_on[p] = (held[0, p] + near[0, p].astype(F32)).astype(BF16)
        far_copy(p).start()

    def analyse(p, _):
        first = ord_ref[here * ORDERS + 2 * p]
        odd_first = first & 1
        e = jnp.where(odd_first == 0, first, DEG - 1 - first)
        rows = jnp.concatenate(
            [
                jnp.concatenate([side[t, half, pl.ds(8 * par + p, 16, stride=16), :] for t in range(TILES)], axis=1)
                for par in range(2)
                for half in range(2)
            ],
            axis=0,
        ).astype(BF16)
        both = lax.dot_general(rows, tab[p], NT, preferred_element_type=F32)
        final = lax.dot_general(rows[32:64], last_ref[p], NT, preferred_element_type=F32)
        final = jnp.where(tiny_even, final[0:16], final[16:32])
        ca = jnp.where(pos_even, both[0:16], both[16:32])
        cb = jnp.where(pos_even, both[32:48], both[48:64])
        ca = jnp.where(pos >= e, pltpu.roll(ca, e, 1), 0.0)
        cb = jnp.concatenate([cb, final, jnp.zeros((16, WIDE - DEG - 16), F32)], axis=1)
        cb = pltpu.roll(cb, WIDE - 1 - (e & 7), 1)[:, 0:DEG]
        cb = jnp.where(pos >= DEG - 1 - e, cb, 0.0)
        keep = jnp.full((16, DEG), odd_first) == 0
        pair = (jnp.where(keep, ca, cb), jnp.where(keep, cb, ca))
        for k in range(2):
            for c in range(COMPS):
                out_ref[c, 0, 2 * p + k] = pair[k][2 * c : 2 * c + 2].astype(BF16)
        scaled = jnp.concatenate([pair[0][0:12], pair[1][0:12]], axis=0) * rad_ref[0]
        for layer_index in range(2):
            for core_index in range(2):
                piece = scaled[:, share * (2 * layer_index + core_index) : share * (2 * layer_index + core_index + 1)]
                is_across = layer_index != layer
                k = jnp.where(is_across, 0, 1)

                @pl.when(core_index == core)
                def _():
                    held[k, p] = piece

                @pl.when(core_index != core)
                def _():
                    part[k, p] = piece.astype(BF16)

        near_copy(0, p).start()
        near_copy(1, p).start()

        @pl.when(p > 0)
        def _():
            forward(p - 1)

        return 0

    lax.fori_loop(0, PAIRS, analyse, 0)
    forward(PAIRS - 1)

    def finish(p, _):
        near_copy(1, p).wait_recv()
        total = held[1, p] + near[1, p].astype(F32)
        far_copy(p).wait_recv()
        total = total + far[p].astype(F32)
        for k in range(2):
            for c in range(COMPS):
                sum_ref[c, 2 * p + k] = total[12 * k + 2 * c : 12 * k + 2 * c + 2]
        near_copy(0, p).wait_send()
        near_copy(1, p).wait_send()
        far_copy(p).wait_send()
        return 0

    lax.fori_loop(0, PAIRS, finish, 0)


def run_whole(order_map, rad, shift, vis, lat, g, spec):
    smem, vmem = pl.BlockSpec(memory_space=pltpu.SMEM), pl.BlockSpec(memory_space=pltpu.VMEM)
    share = DEG // SHELLS
    block = (PAIRS, 24, share)
    return pl.pallas_call(
        whole_kernel,
        in_specs=[smem, smem, vmem, vmem, vmem, vmem, vmem],
        out_specs=[vmem, vmem],
        out_shape=[
            jax.ShapeDtypeStruct((COMPS, 1, ORDERS, PARTS, DEG), BF16),
            jax.ShapeDtypeStruct((COMPS, ORDERS, PARTS, share), F32),
        ],
        scratch_shapes=[
            pltpu.VMEM((PAIRS, DEG, HALF), BF16),
            pltpu.VMEM((PAIRS, 16, HALF), BF16),
            pltpu.VMEM((BLK, 24, 128), BF16),
            pltpu.VMEM((POINTS, KH), BF16),
            pltpu.VMEM((192, POINTS), BF16),
            pltpu.VMEM((192, KH), BF16),
            pltpu.VMEM((CYC, POINTS), F32),
            pltpu.VMEM((BLK, 24, 128), BF16),
            pltpu.VMEM((BLK, 24, 128), BF16),
            pltpu.VMEM((BLK, 24, 128), BF16),
            pltpu.VMEM((TILES, 2, 256, 128), F32),
            pltpu.VMEM((2,) + block, BF16),
            pltpu.VMEM((2,) + block, F32),
            pltpu.VMEM((2,) + block, BF16),
            pltpu.VMEM(block, BF16),
            pltpu.VMEM(block, BF16),
            pltpu.SemaphoreType.DMA((5,)),
            pltpu.SemaphoreType.DMA((3, 2, PAIRS)),
            pltpu.VMEM(((DEG // 128 + 1) * (128 // TURN), 8, 128), F32),
            pltpu.VMEM(((DEG // 128 + 1) * (128 // TURN), 8, 128), F32),
            pltpu.VMEM((TILES, 8, 128), F32),
            pltpu.VMEM((TILES, 8, 128), F32),
            pltpu.VMEM((TILES, 8, 128), F32),
            pltpu.VMEM((TILES, 8, 128), F32),
            pltpu.VMEM((TILES, 8, 128), F32),
            pltpu.VMEM((TILES, 8, 128), F32),
            pltpu.VMEM((8, 128), F32),
            pltpu.VMEM((TURN, 2, 8, 128), F32),
            pltpu.VMEM((TURN, 2, 8, 128), F32),
            pltpu.VMEM((2, TILES, PAIRS * LSTRIDE + 8, 128), F32),
            pltpu.VMEM((PAIRS, 2, 64, 256), F32),
            pltpu.VMEM((PAIRS, 64, WIDE), BF16),
            pltpu.VMEM((2 * TILES, 256, 128), F32),
        ],
        compiler_params=pltpu.CompilerParams(collective_id=0, has_side_effects=True),
        name="whole",
    )(order_map, rad, shift, vis, lat, g, spec)


def shift_table():
    k = np.arange(KH, dtype=np.float64)
    ang = 2.0 * np.pi * k / POINTS
    sign = 1.0 - 2.0 * (k % 2)
    return np.stack([sign * np.cos(ang), sign * np.sin(ang)]).astype(np.float32)


def shards(strain_spec, order_map, viscosity, radial_weight):
    lat, g = latitude_constants()
    lat, g = jnp.asarray(lat), jnp.asarray(g)
    return run_whole(order_map, radial_weight, jnp.asarray(shift_table()), viscosity, lat, g, strain_spec)


def solution(mesh):
    return jax.shard_map(
        shards,
        mesh=mesh,
        in_specs=(P(None, "shell", "blk", None, None), P(), P("shell", "blk", None), P("shell")),
        out_specs=(P(None, "shell", "blk", None, None), P(None, "blk", None, "shell")),
        check_vma=False,
    )
```

```python
import math

import jax
import jax.numpy as jnp
import numpy as np
from jax import lax
from jax.experimental import pallas as pl
from jax.experimental.pallas import tpu as pltpu
from jax.sharding import PartitionSpec as P

F32 = jnp.float32
BF16 = jnp.bfloat16
COMPS = 6
PARTS = 2
ORDERS = 16
DEG = 1024
HALF = 512
BLK = 64
SHELLS = 4
CYC = 16
POINTS = 2048
KH = POINTS // 2
LB = 256
LSTRIDE = LB + 1
TILES = HALF // 128
PAIRS = 8
TURN = 16
TURNS = LB // TURN
WIDE = DEG + 128
BIG = 2.0**40
SMALL = 2.0**-40
NT = (((1,), (1,)), ((), ()))
MESH = pl.DeviceIdType.MESH


def constants():
    j = np.arange(HALF, dtype=np.float64)
    theta = np.pi * (2.0 * j + 1.0) / (4.0 * HALF)
    x = np.cos(theta)
    logsin = np.log2(np.sin(theta))
    hi = np.round(logsin * 512.0) / 512.0
    lo = logsin - hi
    k = np.arange(1, HALF + 1, dtype=np.float64)
    phase = np.outer(k, 2.0 * j + 1.0) % (4.0 * HALF)
    series = np.sum(np.cos(phase * np.pi / (2.0 * HALF)) / (4.0 * k * k - 1.0)[:, None], axis=0)
    weight = (2.0 / (2.0 * HALF)) * (1.0 - 2.0 * series)
    m = np.arange(DEG, dtype=np.float64)
    fac = np.concatenate([[0.0], np.cumsum(np.log2(1.0 - 0.5 / np.arange(1, DEG)))])
    g = 0.5 * np.log2((2.0 * m + 1.0) / (4.0 * np.pi)) + 0.5 * fac
    k = np.arange(KH, dtype=np.float64)
    sign = 1.0 - 2.0 * (k % 2)
    table = np.zeros((8, KH), np.float32)
    table[0:4, 0:HALF] = np.stack([x, hi, lo, weight])
    table[4, 0:DEG] = g
    table[5] = sign * np.cos(2.0 * np.pi * k / POINTS)
    table[6] = sign * np.sin(2.0 * np.pi * k / POINTS)
    return table


def power_of(e):
    return jnp.where(e < -126.0, 0.0, jnp.exp(jnp.maximum(e, -126.0) * math.log(2.0)))


def legendre_init(ord_ref, lat_ref, base, ca, cab, ini, expo, ini2, expo2, mark, bca):
    sub8 = lax.broadcasted_iota(jnp.int32, (8, 128), 0)
    even = jnp.zeros((8, 128), jnp.int32)
    for p in range(PAIRS):
        first = ord_ref[base + 2 * p]
        even = jnp.where(sub8 == p, jnp.where((first & 1) == 0, first, DEG - 1 - first), even)
    ma = even.astype(F32)
    mb = (DEG - 1.0) - ma
    delta = (even & 7).astype(F32) + 1.0
    start = mb + delta
    mark[...] = start
    lane = lax.broadcasted_iota(jnp.int32, (8, 128), 1).astype(F32)
    for b in range(DEG // 128 + 1):
        t = lane + float(128 * b)
        second = t >= start
        m = jnp.where(second, mb, ma)
        l = jnp.where(second, t - delta, t + ma)
        up = (l > m) & (l < DEG - 0.5)
        a2 = (4.0 * l * l - 1.0) / jnp.where(up, (l - m) * (l + m), 1.0)
        a = jnp.where(up, jnp.sqrt(jnp.where(up, a2, 1.0)), 0.0)
        below = l - 1.0
        top = jnp.where(below > m, (below - m) * (below + m), 0.0)
        ab = a * jnp.sqrt(top / jnp.maximum(4.0 * below * below - 1.0, 1.0))
        for k in range(128 // TURN):
            ca[b * (128 // TURN) + k] = pltpu.roll(a, (128 - TURN * k) % 128, 1)
            cab[b * (128 // TURN) + k] = pltpu.roll(ab, (128 - TURN * k) % 128, 1)
    glane = lax.broadcasted_iota(jnp.int32, (8, DEG), 1).astype(F32)
    for m, first, power in ((ma, ini, expo), (mb, ini2, expo2)):
        gm = jnp.sum(jnp.where(glane == m[:, :1], lat_ref[4:5, :], 0.0), axis=1, keepdims=True)
        for t in range(TILES):
            cols = pl.ds(128 * t, 128)
            mh = m * lat_ref[1:2, cols]
            whole = jnp.floor(mh)
            first[t] = jnp.exp(((mh - whole) + m * lat_ref[2:3, cols] + gm) * math.log(2.0))
            power[t] = whole
    for r in range(TURN):
        bca[r, 0] = jnp.broadcast_to(ca[0][:, r : r + 1], (8, 128))
        bca[r, 1] = jnp.broadcast_to(cab[0][:, r : r + 1], (8, 128))


def shift_left(pieces, amount):
    lane = lax.broadcasted_iota(jnp.int32, (16, 128), 1)
    turned_pieces = [pltpu.roll(piece, lax.rem(128 - amount, 128), 1) for piece in pieces]
    return [jnp.where(lane < 128 - amount, a, b) for a, b in zip(turned_pieces[:-1], turned_pieces[1:])]


def place_pairs(ord_ref, spec_ref, base, lhs):
    pos = lax.broadcasted_iota(jnp.int32, (16, 128), 1)
    pos_even = (pos & 1) == 0
    zero = jnp.zeros((16, 128), F32)

    def place(p, _):
        first = ord_ref[base + 2 * p]
        odd_first = first & 1
        e = jnp.where(odd_first == 0, first, DEG - 1 - first)
        delta = (e & 7) + 1
        pads = [jnp.zeros((4, DEG), F32)]
        da = jnp.concatenate([spec_ref[c, 0, 2 * p + odd_first].astype(F32) for c in range(COMPS)] + pads, axis=0)
        db = jnp.concatenate([spec_ref[c, 0, 2 * p + 1 - odd_first].astype(F32) for c in range(COMPS)] + pads, axis=0)
        da = pltpu.roll(da * jnp.where(e == 0, 1.0, 2.0), jnp.where(e == 0, 0, DEG - e), 1)
        db = db * 2.0
        pieces = [zero] + [db[:, 128 * k : 128 * k + 128] for k in range(DEG // 128)] + [zero]
        pieces = shift_left(pieces, 128 - delta)
        for k in range(WIDE // 128):
            cols = pl.ds(128 * k, 128)
            a = jnp.where(pos < DEG - e - 128 * k, da[:, 128 * k : 128 * k + 128], 0.0) if k < DEG // 128 else zero
            b = jnp.where(pos >= DEG - e + (e & 7) - 128 * k, pieces[k], 0.0)
            lhs[p, 0:16, cols] = jnp.where(pos_even, a, 0.0).astype(BF16)
            lhs[p, 16:32, cols] = jnp.where(pos_even, 0.0, a).astype(BF16)
            lhs[p, 32:48, cols] = jnp.where(pos_even, b, 0.0).astype(BF16)
            lhs[p, 48:64, cols] = jnp.where(pos_even, 0.0, b).astype(BF16)
        return 0

    lax.fori_loop(0, PAIRS, place, 0)


def legendre_synthesis(ord_ref, lat_ref, spec_ref, base, tab, tail, msg, loads, refs):
    ca, cab, prev, cur, expo, ini, ini2, expo2, mark, bca, bcb, ft, acc, lhs, ns = refs
    loads[0].wait()
    legendre_init(ord_ref, lat_ref, base, ca, cab, ini, expo, ini2, expo2, mark, bca)
    loads[1].wait()
    place_pairs(ord_ref, spec_ref, base, lhs)
    for t in range(TILES):
        prev[t] = jnp.zeros((8, 128), F32)
        cur[t] = jnp.zeros((8, 128), F32)
    acc[...] = jnp.zeros_like(acc)

    def multiply(block, i):
        rows = pl.ds(i * LSTRIDE, LB)
        half_index = lax.rem(block, 2)
        span = pl.ds(pl.multiple_of(block * LB, LB), LB)
        left = lhs[i, :, span]
        for half in range(2):
            table = jnp.concatenate([ft[half_index, 2 * half, rows, :], ft[half_index, 2 * half + 1, rows, :]], axis=1)
            table = table.astype(BF16)
            tab[i, span, 256 * half : 256 * half + 256] = table
            acc[i, half] += jnp.dot(left, table, preferred_element_type=F32)

    def recur(block, i, turns, opening):
        half_index = lax.rem(block, 2)
        xs = [jnp.broadcast_to(lat_ref[0:1, pl.ds(128 * t, 128)], (8, 128)) for t in range(TILES)]
        ps, cs, scales = [prev[t] for t in range(TILES)], [cur[t] for t in range(TILES)], [None] * TILES
        es = [expo[t] for t in range(TILES)]
        for k in range(turns):
            use, make = (bca, bcb) if k == 0 else (bcb, bca)
            chunk = block * TURNS + 2 * i + k
            av, abv = ca[chunk + 1], cab[chunk + 1]
            for r in range(TURN):
                if r % 8 == 0:
                    now = jnp.full((8, 128), chunk * TURN + r).astype(F32)
                    hit = mark[...] == now
                    for t in range(TILES):
                        big = jnp.abs(cs[t]) > BIG
                        f = jnp.where(big, SMALL, 1.0)
                        es[t] = jnp.where(hit, expo2[t], jnp.where(big, es[t] + 40.0, es[t]))
                        scales[t] = power_of(es[t])
                        ps[t], cs[t] = ps[t] * f, cs[t] * f
                if turns == 2:
                    make[r, 0] = jnp.broadcast_to(av[:, r : r + 1], (8, 128))
                    make[r, 1] = jnp.broadcast_to(abv[:, r : r + 1], (8, 128))
                a, ab = use[r, 0], use[r, 1]
                for t in range(TILES):
                    new = (a * xs[t]) * cs[t] - ab * ps[t]
                    if r % 8 == 0:
                        new = jnp.where(hit, ini2[t], new)
                        if opening and r == 0 and k == 0:
                            new = jnp.where(now == 0.0, ini[t], new)
                    ps[t], cs[t] = cs[t], new
                    ft[half_index, t, pl.ds(2 * TURN * i + TURN * k + r, 8, stride=LSTRIDE), :] = new * scales[t]
        for t in range(TILES):
            prev[t], cur[t], expo[t] = ps[t], cs[t], es[t]

    def first_block(i, _):
        recur(0, i, 2, True)
        return 0

    def middle(n, _):
        block, i = n // PAIRS, lax.rem(n, PAIRS)
        multiply(block - 1, i)
        recur(block, i, 2, False)
        return 0

    lax.fori_loop(0, PAIRS, first_block, 0)
    lax.fori_loop(PAIRS, PAIRS * (DEG // LB), middle, 0)
    recur(DEG // LB, 0, 1, False)

    def last_block(i, _):
        multiply(DEG // LB - 1, i)
        rows = pl.ds(i * LSTRIDE, 16)
        table = jnp.concatenate([ft[0, t, rows, :] for t in range(TILES)], axis=1).astype(BF16)
        tail[i] = table
        extra = jnp.dot(lhs[i, 32:64, DEG:WIDE][:, 0:16], table, preferred_element_type=F32)
        for t in range(TILES):
            cols = slice(128 * (t % 2), 128 * (t % 2) + 128)
            part = acc[i, t // 2]
            for par in range(2):
                sym, anti = part[32 * par : 32 * par + 16, cols], part[32 * par + 16 : 32 * par + 32, cols]
                if par:
                    sym = sym + extra[0:16, 128 * t : 128 * t + 128]
                    anti = anti + extra[16:32, 128 * t : 128 * t + 128]
                ns[t, pl.ds(par * 8 + i, 16, stride=16), :] = sym + anti
                ns[TILES + t, pl.ds(par * 8 + i, 16, stride=16), :] = sym - anti
        return 0

    lax.fori_loop(0, PAIRS, last_block, 0)
    lane = lax.broadcasted_iota(jnp.int32, (8, 128), 1)
    for t in range(2 * TILES):
        near, far = ns[t, 0:128].T, ns[t, 128:256].T
        moved = pltpu.roll(far, 64, 1)
        for b in range(8):
            d = (t % TILES) * 8 + b
            dest = d if t < TILES else BLK - 1 - d
            msg[dest, 0:16] = near[16 * b : 16 * b + 16].astype(BF16)
            msg[dest, 16:24] = jnp.where(lane < 64, far[16 * b : 16 * b + 8], moved[16 * b + 8 : 16 * b + 16]).astype(BF16)


def turn(phase):
    t = phase * (1.0 / KH) - 1.0
    z = t * t
    c = jnp.full_like(z, 0.0)
    s = jnp.full_like(z, 0.0)
    for i in range(8, -1, -1):
        c = c * z + float((-1) ** (i + 1) * math.pi ** (2 * i) / math.factorial(2 * i))
        s = s * z + float((-1) ** (i + 1) * math.pi ** (2 * i + 1) / math.factorial(2 * i + 1))
    return c, s * t


def wrap(value):
    return value - POINTS * jnp.floor(value * (1.0 / POINTS))


def turned(value, quarters):
    return pltpu.roll(value, (32 * quarters) % 128, 1) if quarters % 4 else value


def whole_kernel(
    ord_ref, rad_ref, vis_hbm, lat_hbm, spec_hbm, out_ref, sum_ref,
    lat_ref, spec_ref, vis_ref, tab, last_ref, msg_ref, wave, left, pm, vis, got, give, back, side, part, held, near, coefs, sems, pair_sems, *refs,
):
    here = lax.axis_index("blk")
    shell = lax.axis_index("shell")
    loads = [
        pltpu.make_async_copy(src, dst, sems.at[5 + i])
        for i, (src, dst) in enumerate(((lat_hbm, lat_ref), (spec_hbm, spec_ref), (vis_hbm, vis_ref)))
    ]
    for load in loads:
        load.start()
    barrier = pltpu.get_barrier_semaphore()

    def greet(i, _):
        pl.semaphore_signal(barrier, inc=1, device_id={"blk": lax.rem(here + i, BLK)}, device_id_type=MESH)
        return 0

    lax.fori_loop(1, BLK, greet, 0, unroll=7)
    for i in range(1, SHELLS):
        pl.semaphore_signal(barrier, inc=1, device_id={"shell": lax.rem(shell + i, SHELLS)}, device_id_type=MESH)

    legendre_synthesis(ord_ref, lat_ref, spec_ref, here * ORDERS, tab, last_ref, msg_ref, loads, refs)
    pl.semaphore_wait(barrier, BLK + SHELLS - 2)

    def send_first(i, _):
        peer = lax.rem(here + i, BLK)
        pltpu.make_async_remote_copy(
            src_ref=msg_ref.at[peer], dst_ref=got.at[here], send_sem=sems.at[0], recv_sem=sems.at[1],
            device_id={"blk": peer}, device_id_type=MESH,
        ).start()
        return 0

    lax.fori_loop(1, BLK, send_first, 0, unroll=7)
    own = pltpu.make_async_copy(msg_ref.at[here], got.at[here], sems.at[4])
    own.start()

    lane = lax.broadcasted_iota(jnp.int32, (8, 128), 1).astype(F32)
    sub8 = lax.broadcasted_iota(jnp.int32, (8, 128), 0)
    sc, ss = [], []
    for u in range(KH // 128):
        sc.append(jnp.broadcast_to(lat_ref[5:6, pl.ds(128 * u, 128)], (8, 128)))
        ss.append(jnp.broadcast_to(lat_ref[6:7, pl.ds(128 * u, 128)], (8, 128)))

    def make(src, _):
        even = jnp.zeros((8, 128), jnp.int32)
        for p in range(PAIRS):
            first = ord_ref[src * ORDERS + 2 * p]
            even = jnp.where(sub8 == p, jnp.where((first & 1) == 0, first, DEG - 1 - first), even)
        m = even.astype(F32)
        c, s = turn(wrap(m * lane))
        gc, gs = turn(wrap(m * 128.0))
        for u in range(KH // 128):
            oc = sc[u] * c - ss[u] * s
            os = -(ss[u] * c + sc[u] * s)
            rows = pl.ds(pl.multiple_of(src * 32, 32), 32)
            wave[rows, pl.ds(128 * u, 128)] = jnp.concatenate([c, oc, -s, -os], axis=0).astype(BF16)
            c, s = c * gc - s * gs, s * gc + c * gs
        return 0

    lax.fori_loop(0, BLK, make, 0, unroll=4)
    loads[2].wait()
    for j in range(CYC):
        row = jnp.where(here >= BLK // 2, CYC - 1 - j, j)
        vis[j : j + 1, :] = vis_ref[0, pl.ds(row, 1), :]

    own.wait()
    pltpu.make_async_remote_copy(
        src_ref=msg_ref.at[0 : BLK - 1], dst_ref=got.at[0 : BLK - 1], send_sem=sems.at[0], recv_sem=sems.at[1],
        device_id={"blk": here}, device_id_type=MESH,
    ).wait()

    wide = lax.broadcasted_iota(jnp.int32, (16, 128), 1)
    even = ((wide // 8) % 2) == 0
    quarter = wide // 32
    for g in range(BLK // 4):
        pieces = [(got[4 * g + i, 0:16].astype(F32), got[4 * g + i, 16:24].astype(F32)) for i in range(4)]
        for c in range(COMPS):
            total = None
            for i in range(4):
                first, rest = pieces[i]
                moved = turned(first, i - c) if c < 4 else jnp.concatenate([turned(rest, i - c), turned(rest, i - c - 2)], axis=0)
                total = moved if total is None else jnp.where(quarter == i, moved, total)
            left[16 * c : 16 * c + 16, pl.ds(128 * g, 128)] = jnp.where(even, total, 0.0).astype(BF16)
            left[96 + 16 * c : 112 + 16 * c, pl.ds(128 * g, 128)] = jnp.where(even, 0.0, total).astype(BF16)

    for u in range(KH // 256):
        cols = pl.ds(256 * u, 256)
        field = jnp.dot(left[...], wave[:, cols], preferred_element_type=F32)
        low, high = vis[:, cols], vis[:, pl.ds(KH + 256 * u, 256)]
        for c in range(COMPS):
            e, o = field[16 * c : 16 * c + 16], field[96 + 16 * c : 112 + 16 * c]
            first, second = low * (e + o), high * (e - o)
            pm[16 * c : 16 * c + 16, cols] = (first + second).astype(BF16)
            pm[96 + 16 * c : 112 + 16 * c, cols] = (first - second).astype(BF16)

    lanes = lax.broadcasted_iota(jnp.int32, (96, 256), 1)
    pick = ((lanes // 8) % 2) == 0

    def send_block(blk):
        for i in range(8):
            peer = blk * 8 + i

            @pl.when(peer != here)
            def _():
                pltpu.make_async_remote_copy(
                    src_ref=give.at[peer], dst_ref=back.at[here], send_sem=sems.at[2], recv_sem=sems.at[3],
                    device_id={"blk": peer}, device_id_type=MESH,
                ).start()

    def block_of(b):
        return lax.rem(b + here // 8, 8)

    def spectra(b):
        blk = block_of(b)
        rows = pl.ds(pl.multiple_of(blk * 256, 256), 256)
        both = lax.dot_general(pm[...], wave[rows, :], NT, preferred_element_type=F32)
        spect = jnp.where(pick, both[:96], both[96:]) * (2.0 * math.pi / POINTS)
        for g in range(2):
            vals = [spect[16 * c : 16 * c + 16, 128 * g : 128 * g + 128] for c in range(COMPS)]
            for i in range(4):
                low = None
                for c in range(4):
                    moved = turned(vals[c], c - i)
                    low = moved if low is None else jnp.where(quarter == c, moved, low)
                high = None
                for c in range(4):
                    moved = turned(vals[4 + c % 2][8 * (c // 2) : 8 * (c // 2) + 8], c - i)
                    high = moved if high is None else jnp.where(quarter[:8] == c, moved, high)
                give[blk * 8 + 4 * g + i, 0:16] = low.astype(BF16)
                give[blk * 8 + 4 * g + i, 16:24] = high.astype(BF16)

    def spectra_and_send(b, _):
        send_block(block_of(b + 7))
        spectra(b)
        return 0

    spectra(0)
    lax.fori_loop(1, 8, spectra_and_send, 0)
    send_block(block_of(7))
    own = pltpu.make_async_copy(give.at[here], back.at[here], sems.at[4])
    own.start()
    own.wait()
    pltpu.make_async_remote_copy(
        src_ref=give.at[0 : BLK - 1], dst_ref=back.at[0 : BLK - 1], send_sem=sems.at[2], recv_sem=sems.at[3],
        device_id={"blk": here}, device_id_type=MESH,
    ).wait()

    def fetch(d):
        first, rest = back[d, 0:16].astype(F32), back[d, 16:24].astype(F32)
        return first, jnp.concatenate([rest, pltpu.roll(rest, 64, 1)], axis=0)

    for t in range(TILES):
        w = lat_ref[3:4, pl.ds(128 * t, 128)]
        north = [fetch(8 * t + b) for b in range(8)]
        south = [fetch(BLK - 1 - 8 * t - b) for b in range(8)]
        for h in range(2):
            up = jnp.concatenate([v[h] for v in north], axis=0)
            down = jnp.concatenate([v[h] for v in south], axis=0)
            side[t, 0, pl.ds(128 * h, 128), :] = (up + down).T * w
            side[t, 1, pl.ds(128 * h, 128), :] = (up - down).T * w

    share = DEG // SHELLS
    pos = lax.broadcasted_iota(jnp.int32, (16, DEG), 1)
    pos_even = (pos & 1) == 0
    tiny_even = (lax.broadcasted_iota(jnp.int32, (16, 16), 1) & 1) == 0

    def share_copy(i, p):
        peer = lax.rem(shell + i, SHELLS)
        return pltpu.make_async_remote_copy(
            src_ref=part.at[p, peer], dst_ref=near.at[p, i - 1],
            send_sem=pair_sems.at[0, i - 1, p], recv_sem=pair_sems.at[1, i - 1, p],
            device_id={"shell": peer}, device_id_type=MESH,
        )

    def analyse(p, _):
        first = ord_ref[here * ORDERS + 2 * p]
        odd_first = first & 1
        e = jnp.where(odd_first == 0, first, DEG - 1 - first)
        rows = jnp.concatenate(
            [
                jnp.concatenate([side[t, half, pl.ds(8 * par + p, 16, stride=16), :] for t in range(TILES)], axis=1)
                for par in range(2)
                for half in range(2)
            ],
            axis=0,
        ).astype(BF16)
        both = lax.dot_general(rows, tab[p], NT, preferred_element_type=F32)
        final = lax.dot_general(rows[32:64], last_ref[p], NT, preferred_element_type=F32)
        final = jnp.where(tiny_even, final[0:16], final[16:32])
        ca = jnp.where(pos_even, both[0:16], both[16:32])
        cb = jnp.where(pos_even, both[32:48], both[48:64])
        ca = jnp.where(pos >= e, pltpu.roll(ca, e, 1), 0.0)
        final = jnp.concatenate([final, jnp.zeros((16, 112), F32)], axis=1)
        pieces = [cb[:, 128 * k : 128 * k + 128] for k in range(DEG // 128)] + [final]
        cb = jnp.concatenate(shift_left(pieces, (e & 7) + 1), axis=1)
        cb = jnp.where(pos >= DEG - 1 - e, cb, 0.0)
        keep = jnp.full((16, DEG), odd_first) == 0
        pair = (jnp.where(keep, ca, cb), jnp.where(keep, cb, ca))
        both = jnp.concatenate([pair[0][0:12], pair[1][0:12]], axis=0)
        coefs[p] = both
        scaled = both * rad_ref[0]
        for i in range(SHELLS):
            piece = scaled[:, share * i : share * i + share]
            part[p, i] = piece.astype(BF16)

            @pl.when(shell == i)
            def _():
                held[p] = piece

        for i in (2, 1, 3):
            share_copy(i, p).start()
        return 0

    lax.fori_loop(0, PAIRS, analyse, 0)

    def emit(p, _):
        for k in range(2):
            for c in range(COMPS):
                out_ref[c, 0, 2 * p + k] = coefs[p, 12 * k + 2 * c : 12 * k + 2 * c + 2].astype(BF16)
        return 0

    lax.fori_loop(0, PAIRS, emit, 0)

    def finish(p, _):
        for i in range(1, SHELLS):
            share_copy(i, p).wait()
        total = held[p] + near[p, 0].astype(F32) + near[p, 1].astype(F32) + near[p, 2].astype(F32)
        for k in range(2):
            for c in range(COMPS):
                sum_ref[c, 2 * p + k] = total[12 * k + 2 * c : 12 * k + 2 * c + 2]
        return 0

    lax.fori_loop(0, PAIRS, finish, 0)


def run_whole(order_map, rad, vis, lat, spec):
    smem, vmem = pl.BlockSpec(memory_space=pltpu.SMEM), pl.BlockSpec(memory_space=pltpu.VMEM)
    hbm = pl.BlockSpec(memory_space=pltpu.HBM)
    share = DEG // SHELLS
    return pl.pallas_call(
        whole_kernel,
        in_specs=[smem, smem, hbm, hbm, hbm],
        out_specs=[vmem, vmem],
        out_shape=[
            jax.ShapeDtypeStruct((COMPS, 1, ORDERS, PARTS, DEG), BF16),
            jax.ShapeDtypeStruct((COMPS, ORDERS, PARTS, share), F32),
        ],
        scratch_shapes=[
            pltpu.VMEM((8, KH), F32),
            pltpu.VMEM(spec.shape, BF16),
            pltpu.VMEM(vis.shape, F32),
            pltpu.VMEM((PAIRS, DEG, HALF), BF16),
            pltpu.VMEM((PAIRS, 16, HALF), BF16),
            pltpu.VMEM((BLK, 24, 128), BF16),
            pltpu.VMEM((POINTS, KH), BF16),
            pltpu.VMEM((192, POINTS), BF16),
            pltpu.VMEM((192, KH), BF16),
            pltpu.VMEM((CYC, POINTS), F32),
            pltpu.VMEM((BLK, 24, 128), BF16),
            pltpu.VMEM((BLK, 24, 128), BF16),
            pltpu.VMEM((BLK, 24, 128), BF16),
            pltpu.VMEM((TILES, 2, 256, 128), F32),
            pltpu.VMEM((PAIRS, SHELLS, 24, share), BF16),
            pltpu.VMEM((PAIRS, 24, share), F32),
            pltpu.VMEM((PAIRS, SHELLS - 1, 24, share), BF16),
            pltpu.VMEM((PAIRS, 24, DEG), F32),
            pltpu.SemaphoreType.DMA((8,)),
            pltpu.SemaphoreType.DMA((2, SHELLS - 1, PAIRS)),
            pltpu.VMEM(((DEG // 128 + 1) * (128 // TURN), 8, 128), F32),
            pltpu.VMEM(((DEG // 128 + 1) * (128 // TURN), 8, 128), F32),
            pltpu.VMEM((TILES, 8, 128), F32),
            pltpu.VMEM((TILES, 8, 128), F32),
            pltpu.VMEM((TILES, 8, 128), F32),
            pltpu.VMEM((TILES, 8, 128), F32),
            pltpu.VMEM((TILES, 8, 128), F32),
            pltpu.VMEM((TILES, 8, 128), F32),
            pltpu.VMEM((8, 128), F32),
            pltpu.VMEM((TURN, 2, 8, 128), F32),
            pltpu.VMEM((TURN, 2, 8, 128), F32),
            pltpu.VMEM((2, TILES, PAIRS * LSTRIDE + 8, 128), F32),
            pltpu.VMEM((PAIRS, 2, 64, 256), F32),
            pltpu.VMEM((PAIRS, 64, WIDE), BF16),
            pltpu.VMEM((2 * TILES, 256, 128), F32),
        ],
        compiler_params=pltpu.CompilerParams(collective_id=0, has_side_effects=True, vmem_limit_bytes=48 * 2**20),
        name="whole",
    )(order_map, rad, vis, lat, spec)


def shards(strain_spec, order_map, viscosity, radial_weight):
    stay = lambda x: pltpu.with_memory_space_constraint(x, pltpu.HBM)
    return run_whole(stay(order_map), radial_weight, stay(viscosity), stay(jnp.asarray(constants())), stay(strain_spec))


def solution(mesh):
    return jax.shard_map(
        shards,
        mesh=mesh,
        in_specs=(P(None, "shell", "blk", None, None), P(), P("shell", "blk", None), P("shell")),
        out_specs=(P(None, "shell", "blk", None, None), P(None, "blk", None, "shell")),
        check_vma=False,
    )
```

```python
import math

import jax
import jax.numpy as jnp
import numpy as np
from jax import lax
from jax.experimental import pallas as pl
from jax.experimental.pallas import tpu as pltpu
from jax.sharding import PartitionSpec as P

F32 = jnp.float32
BF16 = jnp.bfloat16
COMPS = 6
PARTS = 2
ORDERS = 16
DEG = 1024
HALF = 512
BLK = 64
SHELLS = 4
CYC = 16
POINTS = 2048
KH = POINTS // 2
LB = 256
LSTRIDE = LB + 1
TILES = HALF // 128
PAIRS = 8
TURN = 16
TURNS = LB // TURN
WIDE = DEG + 128
BIG = 2.0**40
SMALL = 2.0**-40
NT = (((1,), (1,)), ((), ()))
MESH = pl.DeviceIdType.MESH


def constants():
    j = np.arange(HALF, dtype=np.float64)
    theta = np.pi * (2.0 * j + 1.0) / (4.0 * HALF)
    x = np.cos(theta)
    logsin = np.log2(np.sin(theta))
    hi = np.round(logsin * 512.0) / 512.0
    lo = logsin - hi
    k = np.arange(1, HALF + 1, dtype=np.float64)
    phase = np.outer(k, 2.0 * j + 1.0) % (4.0 * HALF)
    series = np.sum(np.cos(phase * np.pi / (2.0 * HALF)) / (4.0 * k * k - 1.0)[:, None], axis=0)
    weight = (2.0 / (2.0 * HALF)) * (1.0 - 2.0 * series)
    m = np.arange(DEG, dtype=np.float64)
    fac = np.concatenate([[0.0], np.cumsum(np.log2(1.0 - 0.5 / np.arange(1, DEG)))])
    g = 0.5 * np.log2((2.0 * m + 1.0) / (4.0 * np.pi)) + 0.5 * fac
    k = np.arange(KH, dtype=np.float64)
    sign = 1.0 - 2.0 * (k % 2)
    table = np.zeros((8, KH), np.float32)
    table[0:4, 0:HALF] = np.stack([x, hi, lo, weight])
    table[4, 0:DEG] = g
    table[5] = sign * np.cos(2.0 * np.pi * k / POINTS)
    table[6] = sign * np.sin(2.0 * np.pi * k / POINTS)
    return table


def power_of(e):
    return jnp.where(e < -126.0, 0.0, jnp.exp(jnp.maximum(e, -126.0) * math.log(2.0)))


def legendre_init(ord_ref, lat_ref, base, ca, cab, ini, expo, ini2, expo2, mark, bca):
    sub8 = lax.broadcasted_iota(jnp.int32, (8, 128), 0)
    even = jnp.zeros((8, 128), jnp.int32)
    for p in range(PAIRS):
        first = ord_ref[base + 2 * p]
        even = jnp.where(sub8 == p, jnp.where((first & 1) == 0, first, DEG - 1 - first), even)
    ma = even.astype(F32)
    mb = (DEG - 1.0) - ma
    delta = (even & 7).astype(F32) + 1.0
    start = mb + delta
    mark[...] = start
    lane = lax.broadcasted_iota(jnp.int32, (8, 128), 1).astype(F32)
    for b in range(DEG // 128 + 1):
        t = lane + float(128 * b)
        second = t >= start
        m = jnp.where(second, mb, ma)
        l = jnp.where(second, t - delta, t + ma)
        up = (l > m) & (l < DEG - 0.5)
        a2 = (4.0 * l * l - 1.0) / jnp.where(up, (l - m) * (l + m), 1.0)
        a = jnp.where(up, jnp.sqrt(jnp.where(up, a2, 1.0)), 0.0)
        below = l - 1.0
        top = jnp.where(below > m, (below - m) * (below + m), 0.0)
        ab = a * jnp.sqrt(top / jnp.maximum(4.0 * below * below - 1.0, 1.0))
        for k in range(128 // TURN):
            ca[b * (128 // TURN) + k] = pltpu.roll(a, (128 - TURN * k) % 128, 1)
            cab[b * (128 // TURN) + k] = pltpu.roll(ab, (128 - TURN * k) % 128, 1)
    glane = lax.broadcasted_iota(jnp.int32, (8, DEG), 1).astype(F32)
    for m, first, power in ((ma, ini, expo), (mb, ini2, expo2)):
        gm = jnp.sum(jnp.where(glane == m[:, :1], lat_ref[4:5, :], 0.0), axis=1, keepdims=True)
        for t in range(TILES):
            cols = pl.ds(128 * t, 128)
            mh = m * lat_ref[1:2, cols]
            whole = jnp.floor(mh)
            first[t] = jnp.exp(((mh - whole) + m * lat_ref[2:3, cols] + gm) * math.log(2.0))
            power[t] = whole
    for r in range(TURN):
        bca[r, 0] = jnp.broadcast_to(ca[0][:, r : r + 1], (8, 128))
        bca[r, 1] = jnp.broadcast_to(cab[0][:, r : r + 1], (8, 128))


def shift_left(pieces, amount):
    lane = lax.broadcasted_iota(jnp.int32, (16, 128), 1)
    turned_pieces = [pltpu.roll(piece, lax.rem(128 - amount, 128), 1) for piece in pieces]
    return [jnp.where(lane < 128 - amount, a, b) for a, b in zip(turned_pieces[:-1], turned_pieces[1:])]


def place_pairs(ord_ref, spec_ref, base, lhs):
    pos = lax.broadcasted_iota(jnp.int32, (16, 128), 1)
    pos_even = (pos & 1) == 0
    zero = jnp.zeros((16, 128), F32)

    def place(p):
        first = ord_ref[base + 2 * p]
        odd_first = first & 1
        e = jnp.where(odd_first == 0, first, DEG - 1 - first)
        delta = (e & 7) + 1
        pads = [jnp.zeros((4, DEG), F32)]
        da = jnp.concatenate([spec_ref[c, 0, 2 * p + odd_first].astype(F32) for c in range(COMPS)] + pads, axis=0)
        db = jnp.concatenate([spec_ref[c, 0, 2 * p + 1 - odd_first].astype(F32) for c in range(COMPS)] + pads, axis=0)
        da = pltpu.roll(da * jnp.where(e == 0, 1.0, 2.0), jnp.where(e == 0, 0, DEG - e), 1)
        db = db * 2.0
        pieces = [zero] + [db[:, 128 * k : 128 * k + 128] for k in range(DEG // 128)] + [zero]
        pieces = shift_left(pieces, 128 - delta)
        for k in range(WIDE // 128):
            cols = pl.ds(128 * k, 128)
            a = jnp.where(pos < DEG - e - 128 * k, da[:, 128 * k : 128 * k + 128], 0.0) if k < DEG // 128 else zero
            b = jnp.where(pos >= DEG - e + (e & 7) - 128 * k, pieces[k], 0.0)
            lhs[p, 0:16, cols] = jnp.where(pos_even, a, 0.0).astype(BF16)
            lhs[p, 16:32, cols] = jnp.where(pos_even, 0.0, a).astype(BF16)
            lhs[p, 32:48, cols] = jnp.where(pos_even, b, 0.0).astype(BF16)
            lhs[p, 48:64, cols] = jnp.where(pos_even, 0.0, b).astype(BF16)

    return place


def legendre_synthesis(ord_ref, lat_ref, spec_ref, base, tab, tail, msg, loads, refs):
    ca, cab, prev, cur, expo, ini, ini2, expo2, mark, bca, bcb, ft, acc, lhs, ns = refs
    loads[0].wait()
    legendre_init(ord_ref, lat_ref, base, ca, cab, ini, expo, ini2, expo2, mark, bca)
    loads[1].wait()
    place = place_pairs(ord_ref, spec_ref, base, lhs)
    for t in range(TILES):
        prev[t] = jnp.zeros((8, 128), F32)
        cur[t] = jnp.zeros((8, 128), F32)
    acc[...] = jnp.zeros_like(acc)

    def multiply(block, i):
        rows = pl.ds(i * LSTRIDE, LB)
        half_index = lax.rem(block, 2)
        span = pl.ds(pl.multiple_of(block * LB, LB), LB)
        left = lhs[i, :, span]
        for half in range(2):
            table = jnp.concatenate([ft[half_index, 2 * half, rows, :], ft[half_index, 2 * half + 1, rows, :]], axis=1)
            table = table.astype(BF16)
            tab[i, span, 256 * half : 256 * half + 256] = table
            acc[i, half] += jnp.dot(left, table, preferred_element_type=F32)

    def recur(block, i, turns, opening):
        half_index = lax.rem(block, 2)
        xs = [jnp.broadcast_to(lat_ref[0:1, pl.ds(128 * t, 128)], (8, 128)) for t in range(TILES)]
        ps, cs, scales = [prev[t] for t in range(TILES)], [cur[t] for t in range(TILES)], [None] * TILES
        es = [expo[t] for t in range(TILES)]
        for k in range(turns):
            use, make = (bca, bcb) if k == 0 else (bcb, bca)
            chunk = block * TURNS + 2 * i + k
            av, abv = ca[chunk + 1], cab[chunk + 1]
            for r in range(TURN):
                if r % 8 == 0:
                    now = jnp.full((8, 128), chunk * TURN + r).astype(F32)
                    hit = mark[...] == now
                    for t in range(TILES):
                        big = jnp.abs(cs[t]) > BIG
                        f = jnp.where(big, SMALL, 1.0)
                        es[t] = jnp.where(hit, expo2[t], jnp.where(big, es[t] + 40.0, es[t]))
                        scales[t] = power_of(es[t])
                        ps[t], cs[t] = ps[t] * f, cs[t] * f
                if turns == 2:
                    make[r, 0] = jnp.broadcast_to(av[:, r : r + 1], (8, 128))
                    make[r, 1] = jnp.broadcast_to(abv[:, r : r + 1], (8, 128))
                a, ab = use[r, 0], use[r, 1]
                for t in range(TILES):
                    new = (a * xs[t]) * cs[t] - ab * ps[t]
                    if r % 8 == 0:
                        new = jnp.where(hit, ini2[t], new)
                        if opening and r == 0 and k == 0:
                            new = jnp.where(now == 0.0, ini[t], new)
                    ps[t], cs[t] = cs[t], new
                    ft[half_index, t, pl.ds(2 * TURN * i + TURN * k + r, 8, stride=LSTRIDE), :] = new * scales[t]
        for t in range(TILES):
            prev[t], cur[t], expo[t] = ps[t], cs[t], es[t]

    def first_block(i, _):
        place(i)
        recur(0, i, 2, True)
        return 0

    def middle(n, _):
        block, i = n // PAIRS, lax.rem(n, PAIRS)
        multiply(block - 1, i)
        recur(block, i, 2, False)
        return 0

    lax.fori_loop(0, PAIRS, first_block, 0)
    lax.fori_loop(PAIRS, PAIRS * (DEG // LB), middle, 0)
    recur(DEG // LB, 0, 1, False)

    def last_block(i, _):
        multiply(DEG // LB - 1, i)
        rows = pl.ds(i * LSTRIDE, 16)
        table = jnp.concatenate([ft[0, t, rows, :] for t in range(TILES)], axis=1).astype(BF16)
        tail[i] = table
        extra = jnp.dot(lhs[i, 32:64, DEG:WIDE][:, 0:16], table, preferred_element_type=F32)
        for t in range(TILES):
            cols = slice(128 * (t % 2), 128 * (t % 2) + 128)
            part = acc[i, t // 2]
            for par in range(2):
                sym, anti = part[32 * par : 32 * par + 16, cols], part[32 * par + 16 : 32 * par + 32, cols]
                if par:
                    sym = sym + extra[0:16, 128 * t : 128 * t + 128]
                    anti = anti + extra[16:32, 128 * t : 128 * t + 128]
                ns[t, pl.ds(par * 8 + i, 16, stride=16), :] = sym + anti
                ns[TILES + t, pl.ds(par * 8 + i, 16, stride=16), :] = sym - anti
        return 0

    lax.fori_loop(0, PAIRS, last_block, 0)
    lane = lax.broadcasted_iota(jnp.int32, (8, 128), 1)
    for t in range(2 * TILES):
        near, far = ns[t, 0:128].T, ns[t, 128:256].T
        moved = pltpu.roll(far, 64, 1)
        for b in range(8):
            d = (t % TILES) * 8 + b
            dest = d if t < TILES else BLK - 1 - d
            msg[dest, 0:16] = near[16 * b : 16 * b + 16].astype(BF16)
            msg[dest, 16:24] = jnp.where(lane < 64, far[16 * b : 16 * b + 8], moved[16 * b + 8 : 16 * b + 16]).astype(BF16)


def turn(phase):
    t = phase * (1.0 / KH) - 1.0
    z = t * t
    c = jnp.full_like(z, 0.0)
    s = jnp.full_like(z, 0.0)
    for i in range(8, -1, -1):
        c = c * z + float((-1) ** (i + 1) * math.pi ** (2 * i) / math.factorial(2 * i))
        s = s * z + float((-1) ** (i + 1) * math.pi ** (2 * i + 1) / math.factorial(2 * i + 1))
    return c, s * t


def wrap(value):
    return value - POINTS * jnp.floor(value * (1.0 / POINTS))


def turned(value, quarters):
    return pltpu.roll(value, (32 * quarters) % 128, 1) if quarters % 4 else value


def whole_kernel(
    ord_ref, rad_ref, vis_hbm, lat_hbm, spec_hbm, out_ref, sum_ref,
    lat_ref, spec_ref, vis_ref, tab, last_ref, msg_ref, wave, left, pm, vis, got, give, back, side, part, held, near, coefs, sems, pair_sems, *refs,
):
    here = lax.axis_index("blk")
    shell = lax.axis_index("shell")
    loads = [
        pltpu.make_async_copy(src, dst, sems.at[5 + i])
        for i, (src, dst) in enumerate(((lat_hbm, lat_ref), (spec_hbm, spec_ref), (vis_hbm, vis_ref)))
    ]
    for load in loads:
        load.start()
    barrier = pltpu.get_barrier_semaphore()

    def greet(i, _):
        pl.semaphore_signal(barrier, inc=1, device_id={"blk": lax.rem(here + i, BLK)}, device_id_type=MESH)
        return 0

    lax.fori_loop(1, BLK, greet, 0, unroll=7)
    for i in range(1, SHELLS):
        pl.semaphore_signal(barrier, inc=1, device_id={"shell": lax.rem(shell + i, SHELLS)}, device_id_type=MESH)

    legendre_synthesis(ord_ref, lat_ref, spec_ref, here * ORDERS, tab, last_ref, msg_ref, loads, refs)
    pl.semaphore_wait(barrier, BLK + SHELLS - 2)

    def send_first(i, _):
        peer = lax.rem(here + i, BLK)
        pltpu.make_async_remote_copy(
            src_ref=msg_ref.at[peer], dst_ref=got.at[here], send_sem=sems.at[0], recv_sem=sems.at[1],
            device_id={"blk": peer}, device_id_type=MESH,
        ).start()
        return 0

    lax.fori_loop(1, BLK, send_first, 0, unroll=7)
    own = pltpu.make_async_copy(msg_ref.at[here], got.at[here], sems.at[4])
    own.start()

    lane = lax.broadcasted_iota(jnp.int32, (8, 128), 1).astype(F32)
    sub8 = lax.broadcasted_iota(jnp.int32, (8, 128), 0)
    sc, ss = [], []
    for u in range(KH // 128):
        sc.append(jnp.broadcast_to(lat_ref[5:6, pl.ds(128 * u, 128)], (8, 128)))
        ss.append(jnp.broadcast_to(lat_ref[6:7, pl.ds(128 * u, 128)], (8, 128)))

    def make(src, _):
        even = jnp.zeros((8, 128), jnp.int32)
        for p in range(PAIRS):
            first = ord_ref[src * ORDERS + 2 * p]
            even = jnp.where(sub8 == p, jnp.where((first & 1) == 0, first, DEG - 1 - first), even)
        m = even.astype(F32)
        c, s = turn(wrap(m * lane))
        gc, gs = turn(wrap(m * 128.0))
        for u in range(KH // 128):
            oc = sc[u] * c - ss[u] * s
            os = -(ss[u] * c + sc[u] * s)
            rows = pl.ds(pl.multiple_of(src * 32, 32), 32)
            wave[rows, pl.ds(128 * u, 128)] = jnp.concatenate([c, oc, -s, -os], axis=0).astype(BF16)
            c, s = c * gc - s * gs, s * gc + c * gs
        return 0

    lax.fori_loop(0, BLK, make, 0, unroll=4)
    loads[2].wait()
    for j in range(CYC):
        row = jnp.where(here >= BLK // 2, CYC - 1 - j, j)
        vis[j : j + 1, :] = vis_ref[0, pl.ds(row, 1), :]

    own.wait()
    pltpu.make_async_remote_copy(
        src_ref=msg_ref.at[0 : BLK - 1], dst_ref=got.at[0 : BLK - 1], send_sem=sems.at[0], recv_sem=sems.at[1],
        device_id={"blk": here}, device_id_type=MESH,
    ).wait()

    wide = lax.broadcasted_iota(jnp.int32, (16, 128), 1)
    even = ((wide // 8) % 2) == 0
    quarter = wide // 32
    for g in range(BLK // 4):
        pieces = [(got[4 * g + i, 0:16].astype(F32), got[4 * g + i, 16:24].astype(F32)) for i in range(4)]
        for c in range(COMPS):
            total = None
            for i in range(4):
                first, rest = pieces[i]
                moved = turned(first, i - c) if c < 4 else jnp.concatenate([turned(rest, i - c), turned(rest, i - c - 2)], axis=0)
                total = moved if total is None else jnp.where(quarter == i, moved, total)
            left[16 * c : 16 * c + 16, pl.ds(128 * g, 128)] = jnp.where(even, total, 0.0).astype(BF16)
            left[96 + 16 * c : 112 + 16 * c, pl.ds(128 * g, 128)] = jnp.where(even, 0.0, total).astype(BF16)

    for u in range(KH // 256):
        cols = pl.ds(256 * u, 256)
        field = jnp.dot(left[...], wave[:, cols], preferred_element_type=F32)
        low, high = vis[:, cols], vis[:, pl.ds(KH + 256 * u, 256)]
        for c in range(COMPS):
            e, o = field[16 * c : 16 * c + 16], field[96 + 16 * c : 112 + 16 * c]
            first, second = low * (e + o), high * (e - o)
            pm[16 * c : 16 * c + 16, cols] = (first + second).astype(BF16)
            pm[96 + 16 * c : 112 + 16 * c, cols] = (first - second).astype(BF16)

    lanes = lax.broadcasted_iota(jnp.int32, (96, 256), 1)
    pick = ((lanes // 8) % 2) == 0

    def send_block(blk):
        for i in range(8):
            peer = blk * 8 + i

            @pl.when(peer != here)
            def _():
                pltpu.make_async_remote_copy(
                    src_ref=give.at[peer], dst_ref=back.at[here], send_sem=sems.at[2], recv_sem=sems.at[3],
                    device_id={"blk": peer}, device_id_type=MESH,
                ).start()

    def block_of(b):
        return lax.rem(b + here // 8, 8)

    def spectra(b):
        blk = block_of(b)
        rows = pl.ds(pl.multiple_of(blk * 256, 256), 256)
        both = lax.dot_general(pm[...], wave[rows, :], NT, preferred_element_type=F32)
        spect = jnp.where(pick, both[:96], both[96:]) * (2.0 * math.pi / POINTS)
        for g in range(2):
            vals = [spect[16 * c : 16 * c + 16, 128 * g : 128 * g + 128] for c in range(COMPS)]
            for i in range(4):
                low = None
                for c in range(4):
                    moved = turned(vals[c], c - i)
                    low = moved if low is None else jnp.where(quarter == c, moved, low)
                high = None
                for c in range(4):
                    moved = turned(vals[4 + c % 2][8 * (c // 2) : 8 * (c // 2) + 8], c - i)
                    high = moved if high is None else jnp.where(quarter[:8] == c, moved, high)
                give[blk * 8 + 4 * g + i, 0:16] = low.astype(BF16)
                give[blk * 8 + 4 * g + i, 16:24] = high.astype(BF16)

    def spectra_and_send(b, _):
        send_block(block_of(b + 7))
        spectra(b)
        return 0

    spectra(0)
    lax.fori_loop(1, 8, spectra_and_send, 0)
    send_block(block_of(7))
    own = pltpu.make_async_copy(give.at[here], back.at[here], sems.at[4])
    own.start()
    own.wait()
    pltpu.make_async_remote_copy(
        src_ref=give.at[0 : BLK - 1], dst_ref=back.at[0 : BLK - 1], send_sem=sems.at[2], recv_sem=sems.at[3],
        device_id={"blk": here}, device_id_type=MESH,
    ).wait()

    def fetch(d):
        first, rest = back[d, 0:16].astype(F32), back[d, 16:24].astype(F32)
        return first, jnp.concatenate([rest, pltpu.roll(rest, 64, 1)], axis=0)

    for t in range(TILES):
        w = lat_ref[3:4, pl.ds(128 * t, 128)]
        north = [fetch(8 * t + b) for b in range(8)]
        south = [fetch(BLK - 1 - 8 * t - b) for b in range(8)]
        for h in range(2):
            up = jnp.concatenate([v[h] for v in north], axis=0)
            down = jnp.concatenate([v[h] for v in south], axis=0)
            side[t, 0, pl.ds(128 * h, 128), :] = (up + down).T * w
            side[t, 1, pl.ds(128 * h, 128), :] = (up - down).T * w

    share = DEG // SHELLS
    pos = lax.broadcasted_iota(jnp.int32, (16, DEG), 1)
    pos_even = (pos & 1) == 0
    tiny_even = (lax.broadcasted_iota(jnp.int32, (16, 16), 1) & 1) == 0

    def share_copy(i, p):
        peer = lax.rem(shell + i, SHELLS)
        return pltpu.make_async_remote_copy(
            src_ref=part.at[p, peer], dst_ref=near.at[p, i - 1],
            send_sem=pair_sems.at[0, i - 1, p], recv_sem=pair_sems.at[1, i - 1, p],
            device_id={"shell": peer}, device_id_type=MESH,
        )

    def analyse(p, _):
        first = ord_ref[here * ORDERS + 2 * p]
        odd_first = first & 1
        e = jnp.where(odd_first == 0, first, DEG - 1 - first)
        rows = jnp.concatenate(
            [
                jnp.concatenate([side[t, half, pl.ds(8 * par + p, 16, stride=16), :] for t in range(TILES)], axis=1)
                for par in range(2)
                for half in range(2)
            ],
            axis=0,
        ).astype(BF16)
        both = lax.dot_general(rows, tab[p], NT, preferred_element_type=F32)
        final = lax.dot_general(rows[32:64], last_ref[p], NT, preferred_element_type=F32)
        final = jnp.where(tiny_even, final[0:16], final[16:32])
        ca = jnp.where(pos_even, both[0:16], both[16:32])
        cb = jnp.where(pos_even, both[32:48], both[48:64])
        ca = jnp.where(pos >= e, pltpu.roll(ca, e, 1), 0.0)
        final = jnp.concatenate([final, jnp.zeros((16, 112), F32)], axis=1)
        pieces = [cb[:, 128 * k : 128 * k + 128] for k in range(DEG // 128)] + [final]
        cb = jnp.concatenate(shift_left(pieces, (e & 7) + 1), axis=1)
        cb = jnp.where(pos >= DEG - 1 - e, cb, 0.0)
        keep = jnp.full((16, DEG), odd_first) == 0
        pair = (jnp.where(keep, ca, cb), jnp.where(keep, cb, ca))
        both = jnp.concatenate([pair[0][0:12], pair[1][0:12]], axis=0)
        coefs[p] = both
        scaled = both * rad_ref[0]
        for i in range(SHELLS):
            piece = scaled[:, share * i : share * i + share]
            part[p, i] = piece.astype(BF16)

            @pl.when(shell == i)
            def _():
                held[p] = piece

        for i in (2, 1, 3):
            share_copy(i, p).start()
        return 0

    lax.fori_loop(0, PAIRS, analyse, 0)

    def emit(p, _):
        for k in range(2):
            for c in range(COMPS):
                out_ref[c, 0, 2 * p + k] = coefs[p, 12 * k + 2 * c : 12 * k + 2 * c + 2].astype(BF16)
        return 0

    lax.fori_loop(0, PAIRS, emit, 0)

    def finish(p, _):
        for i in range(1, SHELLS):
            share_copy(i, p).wait()
        total = held[p] + near[p, 0].astype(F32) + near[p, 1].astype(F32) + near[p, 2].astype(F32)
        for k in range(2):
            for c in range(COMPS):
                sum_ref[c, 2 * p + k] = total[12 * k + 2 * c : 12 * k + 2 * c + 2]
        return 0

    lax.fori_loop(0, PAIRS, finish, 0)


def run_whole(order_map, rad, vis, lat, spec):
    smem, vmem = pl.BlockSpec(memory_space=pltpu.SMEM), pl.BlockSpec(memory_space=pltpu.VMEM)
    hbm = pl.BlockSpec(memory_space=pltpu.HBM)
    share = DEG // SHELLS
    return pl.pallas_call(
        whole_kernel,
        in_specs=[smem, smem, hbm, hbm, hbm],
        out_specs=[vmem, vmem],
        out_shape=[
            jax.ShapeDtypeStruct((COMPS, 1, ORDERS, PARTS, DEG), BF16),
            jax.ShapeDtypeStruct((COMPS, ORDERS, PARTS, share), F32),
        ],
        scratch_shapes=[
            pltpu.VMEM((8, KH), F32),
            pltpu.VMEM(spec.shape, BF16),
            pltpu.VMEM(vis.shape, F32),
            pltpu.VMEM((PAIRS, DEG, HALF), BF16),
            pltpu.VMEM((PAIRS, 16, HALF), BF16),
            pltpu.VMEM((BLK, 24, 128), BF16),
            pltpu.VMEM((POINTS, KH), BF16),
            pltpu.VMEM((192, POINTS), BF16),
            pltpu.VMEM((192, KH), BF16),
            pltpu.VMEM((CYC, POINTS), F32),
            pltpu.VMEM((BLK, 24, 128), BF16),
            pltpu.VMEM((BLK, 24, 128), BF16),
            pltpu.VMEM((BLK, 24, 128), BF16),
            pltpu.VMEM((TILES, 2, 256, 128), F32),
            pltpu.VMEM((PAIRS, SHELLS, 24, share), BF16),
            pltpu.VMEM((PAIRS, 24, share), F32),
            pltpu.VMEM((PAIRS, SHELLS - 1, 24, share), BF16),
            pltpu.VMEM((PAIRS, 24, DEG), F32),
            pltpu.SemaphoreType.DMA((8,)),
            pltpu.SemaphoreType.DMA((2, SHELLS - 1, PAIRS)),
            pltpu.VMEM(((DEG // 128 + 1) * (128 // TURN), 8, 128), F32),
            pltpu.VMEM(((DEG // 128 + 1) * (128 // TURN), 8, 128), F32),
            pltpu.VMEM((TILES, 8, 128), F32),
            pltpu.VMEM((TILES, 8, 128), F32),
            pltpu.VMEM((TILES, 8, 128), F32),
            pltpu.VMEM((TILES, 8, 128), F32),
            pltpu.VMEM((TILES, 8, 128), F32),
            pltpu.VMEM((TILES, 8, 128), F32),
            pltpu.VMEM((8, 128), F32),
            pltpu.VMEM((TURN, 2, 8, 128), F32),
            pltpu.VMEM((TURN, 2, 8, 128), F32),
            pltpu.VMEM((2, TILES, PAIRS * LSTRIDE + 8, 128), F32),
            pltpu.VMEM((PAIRS, 2, 64, 256), F32),
            pltpu.VMEM((PAIRS, 64, WIDE), BF16),
            pltpu.VMEM((2 * TILES, 256, 128), F32),
        ],
        compiler_params=pltpu.CompilerParams(collective_id=0, has_side_effects=True, vmem_limit_bytes=48 * 2**20),
        name="whole",
    )(order_map, rad, vis, lat, spec)


def shards(strain_spec, order_map, viscosity, radial_weight):
    stay = lambda x: pltpu.with_memory_space_constraint(x, pltpu.HBM)
    return run_whole(stay(order_map), radial_weight, stay(viscosity), stay(jnp.asarray(constants())), stay(strain_spec))


def solution(mesh):
    return jax.shard_map(
        shards,
        mesh=mesh,
        in_specs=(P(None, "shell", "blk", None, None), P(), P("shell", "blk", None), P("shell")),
        out_specs=(P(None, "shell", "blk", None, None), P(None, "blk", None, "shell")),
        check_vma=False,
    )
```
